32 devices in a mesh: seq: 4 (over z), exp: 2 (over core), hid: 4 (over y, x).
Axes of the slice: x: 2, y: 2, z: 4, core: 2. Of those that a mesh axis runs over, the one named last changes fastest.
Arguments:
- tokens: bfloat16 [512, 6144], P('seq'), may hold values from -6 to 6
- out_grad: bfloat16 [512, 6144], P('seq'), may hold values from -3 to 3
- expert_ids: int32 [512, 2], P('seq'), may hold values from 0 to 7, as said below
- gate_probs: float32 [512, 2], P('seq'), may hold values from 0.1 to 1
- w_gate: bfloat16 [2, 6144, 16384], P('exp', None, ('seq', 'hid')), may hold values from -0.078125 to 0.078125
- w_up: bfloat16 [2, 6144, 16384], P('exp', None, ('seq', 'hid')), may hold values from -0.078125 to 0.078125
- w_down: bfloat16 [2, 16384, 6144], P('exp', ('seq', 'hid')), may hold values from -0.046875 to 0.046875
Outputs:
- d_w_gate: bfloat16 [2, 6144, 16384], P('exp', None, ('seq', 'hid'))
- d_w_up: bfloat16 [2, 6144, 16384], P('exp', None, ('seq', 'hid'))
- d_w_down: bfloat16 [2, 16384, 6144], P('exp', ('seq', 'hid'))
- d_tokens: float32 [512, 6144], P('seq', 'hid')
- d_gates: float32 [512, 2], P('seq')
The draws below stay inside these ranges and needn't reach their ends.
Inputs may be any that keep to these rules, and one draw needn't show every extreme that they name: `expert_ids`: in each block of 128 rows (the tokens of one index of seq) the two ids of a row differ and no expert is named more than 40 times; each expert below 2 is named 40 // 2 to 40 times in a block, exactly 40 times in the first block.
All inputs are finite; a program needn't handle non-finite values.
Results may differ from the reference program's by a relative error of at most 0.015.
Values may be sent and summed in bfloat16 or wider, within the bound.
No kernel may reach another device: no remote copies, remote signals or barrier semaphores. Data moves between devices by JAX's collectives and lax.ppermute only.
A program may use at most 192 MiB of HBM per device.

```python
import jax
import jax.numpy as jnp
import numpy as np
from jax import lax

D = 6144
FF = 16384
N_EXPERTS = 8
TOPK = 2
TOK_DEV = 128
CAP_DEV = 40
TOKENS = 512
CAPACITY = 160
WIN_EXP = 2
N_SEQ = 4


def draw_expert_ids(key, part):
    blocks = TOKENS // TOK_DEV
    others = N_EXPERTS - WIN_EXP
    half_others = others // 2
    order_list = [0] + list(range(2, 2 + half_others)) + [1] + list(range(2 + half_others, N_EXPERTS))
    order_table = jnp.asarray(np.array(order_list, dtype=np.int32))

    def one_block(block_key, block_index):
        key_count, key_perm, key_flip, key_turn = jax.random.split(block_key, 4)
        window_counts = jax.random.randint(key_count, (WIN_EXP,), CAP_DEV // 2, CAP_DEV + 1).astype(jnp.int32)
        window_counts = jnp.where(block_index == 0, CAP_DEV, window_counts).astype(jnp.int32)
        remain = 2 * TOK_DEV - jnp.sum(window_counts)
        other_index = jnp.arange(others, dtype=jnp.int32)
        other_counts = (remain // others + (other_index < remain % others).astype(jnp.int32)).astype(jnp.int32)
        all_counts = jnp.concatenate([window_counts, other_counts])
        ordered_counts = all_counts[order_table]
        ends = jnp.cumsum(ordered_counts).astype(jnp.int32)
        position = jnp.arange(2 * TOK_DEV, dtype=jnp.int32)
        turn = jax.random.randint(key_turn, (), 0, 2 * TOK_DEV).astype(jnp.int32)
        moved = (position + turn) % (2 * TOK_DEV)
        rank = jnp.sum((moved[:, None] >= ends[None, :]).astype(jnp.int32), axis=1)
        labels = order_table[rank]
        pairs = jnp.stack([labels[:TOK_DEV], labels[TOK_DEV:]], axis=1)
        perm = jax.random.permutation(key_perm, TOK_DEV)
        pairs = pairs[perm]
        flip = jax.random.randint(key_flip, (TOK_DEV, 1), 0, 2)
        pairs = jnp.where(flip == 1, pairs[:, ::-1], pairs)
        return pairs.astype(jnp.int32)
    block_keys = jax.random.split(jax.random.fold_in(key, 17), blocks)
    result = jax.vmap(one_block)(block_keys, jnp.arange(blocks, dtype=jnp.int32))
    return result.reshape(TOKENS, 2).astype(jnp.int32)


def levels(own_key, extent, shards, smallest, high):
    def one(axis_at, blocks):
        draws = jax.random.uniform(jax.random.fold_in(jax.random.fold_in(own_key, 6), axis_at), (blocks,), jnp.float32, smallest / len(shards), high / len(shards))
        return jnp.repeat(jnp.exp(draws), extent[axis_at] // blocks).reshape((-1,) + (1,) * (len(extent) - axis_at - 1))

    level = one(*shards[0])
    for cut in shards[1:]:
        level = level * one(*cut)
    return level


def gaussian(rng, shape, width, most, pieces=(), kind=jnp.bfloat16):
    factor_of = levels(rng, shape, pieces, -0.22, 0.18) if pieces else 1.0
    values = jax.random.normal(rng, shape, jnp.float32) * width * factor_of
    return jnp.minimum(jnp.maximum(values, -most), most).astype(kind)


def setup_inputs(seed: int = 0) -> dict:
    key_list = jax.random.split(jax.random.key(seed), 8)
    tokens = gaussian(key_list[0], (TOKENS, D), 1.0, 6.0, ((0, 4),))
    out_grad = gaussian(key_list[1], (TOKENS, D), 0.5, 3.0, ((0, 4),))
    expert_ids = draw_expert_ids(jax.random.fold_in(key_list[7], 71), 0)
    gate_probs = jnp.clip(0.1 + 0.9 * jax.random.uniform(key_list[3], (TOKENS, TOPK), jnp.float32) ** levels(key_list[3], (TOKENS, TOPK), ((0, 4),), -0.2, 0.2), 0.1, 1.0)
    w_gate = gaussian(key_list[4], (WIN_EXP, D, FF), D ** -0.5, 0.078125, ((0, 2), (2, 16)))
    w_up = gaussian(key_list[5], (WIN_EXP, D, FF), D ** -0.5, 0.078125, ((0, 2), (2, 16)))
    w_down = gaussian(key_list[6], (WIN_EXP, FF, D), FF ** -0.5, 0.046875, ((0, 2), (1, 16)))
    return dict(tokens=tokens, out_grad=out_grad, expert_ids=expert_ids, gate_probs=gate_probs, w_gate=w_gate, w_up=w_up, w_down=w_down)


def pick_rows(expert_ids, expert):
    chosen = (expert_ids.reshape(N_SEQ, TOK_DEV * 2) == expert).astype(jnp.int32)
    slot_index = (jnp.cumsum(chosen, axis=1) - 1).astype(jnp.int32)
    columns = jnp.arange(CAP_DEV, dtype=jnp.int32)
    table = ((chosen[:, :, None] == 1) & (slot_index[:, :, None] == columns[None, None, :])).astype(jnp.float32)
    return table.reshape(N_SEQ, TOK_DEV, 2, CAP_DEV)


def reference(tokens, out_grad, expert_ids, gate_probs, w_gate, w_up, w_down):
    hip = lax.Precision.HIGHEST
    grad_gate_list = []
    grad_up_list = []
    grad_down_list = []
    token_total = jnp.zeros((N_SEQ, TOK_DEV, D), jnp.float32)
    gate_total = jnp.zeros((N_SEQ, TOK_DEV, 2), jnp.float32)
    tok_blocks = tokens.reshape(N_SEQ, TOK_DEV, D).astype(jnp.float32)
    grad_blocks = out_grad.reshape(N_SEQ, TOK_DEV, D).astype(jnp.float32)
    prob_blocks = gate_probs.reshape(N_SEQ, TOK_DEV, 2).astype(jnp.float32)
    for expert in range(WIN_EXP):
        table = pick_rows(expert_ids, expert)
        select_rows = jnp.sum(table, axis=2)
        rows_e = jnp.einsum("stc,std->scd", select_rows, tok_blocks, precision=hip).astype(jnp.bfloat16).reshape(CAPACITY, D)
        grads_e = jnp.einsum("stc,std->scd", select_rows, grad_blocks, precision=hip).astype(jnp.bfloat16).reshape(CAPACITY, D)
        weight_e = jnp.einsum("stkc,stk->sc", table, prob_blocks, precision=hip).reshape(CAPACITY)
        gate_pre = jnp.dot(rows_e, w_gate[expert], preferred_element_type=jnp.float32)
        up_pre = jnp.dot(rows_e, w_up[expert], preferred_element_type=jnp.float32)
        sig_gate = jax.nn.sigmoid(gate_pre)
        activated = gate_pre * sig_gate
        hidden = (activated * up_pre).astype(jnp.bfloat16)
        back_hidden = jnp.dot(grads_e, w_down[expert].T, preferred_element_type=jnp.float32)
        slot_grad = jnp.sum(hidden.astype(jnp.float32) * back_hidden, axis=1)
        weighted = (weight_e[:, None] * hidden.astype(jnp.float32)).astype(jnp.bfloat16)
        grad_down_list.append(jnp.dot(weighted.T, grads_e, preferred_element_type=jnp.float32).astype(jnp.bfloat16))
        scaled_back = weight_e[:, None] * back_hidden
        d_gate = (scaled_back * up_pre * (sig_gate * (1.0 + gate_pre * (1.0 - sig_gate)))).astype(jnp.bfloat16)
        d_up = (scaled_back * activated).astype(jnp.bfloat16)
        grad_gate_list.append(jnp.dot(rows_e.T, d_gate, preferred_element_type=jnp.float32).astype(jnp.bfloat16))
        grad_up_list.append(jnp.dot(rows_e.T, d_up, preferred_element_type=jnp.float32).astype(jnp.bfloat16))
        row_grad = jnp.dot(d_gate, w_gate[expert].T, preferred_element_type=jnp.float32) + jnp.dot(d_up, w_up[expert].T, preferred_element_type=jnp.float32)
        token_total = token_total + jnp.einsum("stc,scd->std", select_rows, row_grad.reshape(N_SEQ, CAP_DEV, D), precision=hip)
        gate_total = gate_total + jnp.einsum("stkc,sc->stk", table, slot_grad.reshape(N_SEQ, CAP_DEV), precision=hip)
    d_tokens = token_total.reshape(TOKENS, D)
    d_gates = gate_total.reshape(TOKENS, 2)
    return (jnp.stack(grad_gate_list), jnp.stack(grad_up_list), jnp.stack(grad_down_list), d_tokens, d_gates)
```

```python
import jax
import jax.numpy as jnp
from jax import lax
from jax.sharding import PartitionSpec as P


def swap(x, axis, bits):
    size = lax.axis_size(axis)
    return lax.ppermute(x, axis, [(i, i ^ bits) for i in range(size)])


def pick_of(expert_ids, expert, capacity):
    tok_rows = expert_ids.shape[0]
    chosen = (expert_ids == expert).astype(jnp.int32)
    slot_index = (jnp.cumsum(chosen.reshape(-1)) - 1).reshape(tok_rows, 2)
    columns = jnp.arange(capacity, dtype=jnp.int32)
    return (
        (chosen[:, :, None] == 1) & (slot_index[:, :, None] == columns[None, None, :])
    ).astype(jnp.float32)


def on_device(tokens, out_grad, expert_ids, gate_probs, w_gate, w_up, w_down):
    expert = lax.axis_index("exp")
    hid = lax.axis_index("hid")
    tok_rows, model_width = tokens.shape
    capacity = 5 * tok_rows // 16
    seq_count = lax.axis_size("seq")
    hid_count = lax.axis_size("hid")
    piece = model_width // hid_count
    bf16, f32 = jnp.bfloat16, jnp.float32
    contract_rows = (((0,), (0,)), ((), ()))

    pick_own = pick_of(expert_ids, expert, capacity)
    pick_other = pick_of(expert_ids, 1 - expert, capacity)
    select_own = jnp.sum(pick_own, axis=1).astype(bf16)
    select_other = jnp.sum(pick_other, axis=1).astype(bf16)
    weight_own = jnp.sum(pick_own * gate_probs[:, :, None], axis=(0, 1))

    def slots_of(x):
        return lax.dot_general(
            select_own, x, contract_rows, preferred_element_type=f32
        ).astype(bf16)

    def quarter(x):
        return lax.dynamic_slice_in_dim(x, hid * piece, piece, axis=1)

    message = jnp.concatenate([slots_of(quarter(tokens)), slots_of(quarter(out_grad))], axis=0)
    arrived = [swap(message, "seq", k) for k in range(1, seq_count)]
    weight_box = jnp.broadcast_to(weight_own[None, :], (8, capacity))
    weights = [weight_own] + [swap(weight_box, "seq", k)[0] for k in range(1, seq_count)]
    weight_e = jnp.concatenate(weights)

    own_rows = slots_of(tokens)
    own_grads = slots_of(out_grad)
    row_pieces = [[] for _ in range(hid_count)]
    grad_pieces = [[] for _ in range(hid_count)]
    for block in arrived:
        row_pieces[0].append(block[:capacity])
        grad_pieces[0].append(block[capacity:])
        if hid_count == 4:
            one = swap(block, "hid", 1)
            two = swap(block, "hid", 2)
            three_rows = swap(one[:capacity], "hid", 2)
            three_grads = swap(two[capacity:], "hid", 1)
            got = [one, two, None]
            row_pieces[1].append(one[:capacity])
            grad_pieces[1].append(one[capacity:])
            row_pieces[2].append(two[:capacity])
            grad_pieces[2].append(two[capacity:])
            row_pieces[3].append(three_rows)
            grad_pieces[3].append(three_grads)
        else:
            for j in range(1, hid_count):
                other = swap(block, "hid", j)
                row_pieces[j].append(other[:capacity])
                grad_pieces[j].append(other[capacity:])

    def whole(own, pieces):
        rest = jnp.zeros(((seq_count - 1) * capacity, model_width), bf16)
        for j in range(hid_count):
            rest = lax.dynamic_update_slice_in_dim(
                rest, jnp.concatenate(pieces[j], axis=0), (hid ^ j) * piece, axis=1
            )
        return jnp.concatenate([own, rest], axis=0)

    rows_e = whole(own_rows, row_pieces)
    grads_e = whole(own_grads, grad_pieces)

    gate_mat, up_mat, down_mat = w_gate[0], w_up[0], w_down[0]
    gate_pre = jnp.dot(rows_e, gate_mat, preferred_element_type=f32)
    up_pre = jnp.dot(rows_e, up_mat, preferred_element_type=f32)
    sig_gate = jax.nn.sigmoid(gate_pre)
    activated = gate_pre * sig_gate
    hidden = (activated * up_pre).astype(bf16)
    back_hidden = lax.dot_general(
        grads_e, down_mat, (((1,), (1,)), ((), ())), preferred_element_type=f32
    )
    slot_part = jnp.sum(hidden.astype(f32) * back_hidden, axis=1)
    weighted = (weight_e[:, None] * hidden.astype(f32)).astype(bf16)
    scaled_back = weight_e[:, None] * back_hidden
    d_gate = (scaled_back * up_pre * (sig_gate * (1.0 + gate_pre * (1.0 - sig_gate)))).astype(bf16)
    d_up = (scaled_back * activated).astype(bf16)

    contract_last = (((1,), (1,)), ((), ()))

    def partial_of(j):
        start = (hid ^ j) * piece
        gate_part = lax.dynamic_slice_in_dim(gate_mat, start, piece, axis=0)
        up_part = lax.dynamic_slice_in_dim(up_mat, start, piece, axis=0)
        return lax.dot_general(
            d_gate, gate_part, contract_last, preferred_element_type=f32
        ) + lax.dot_general(d_up, up_part, contract_last, preferred_element_type=f32)

    received = [
        swap(partial_of(j).astype(bf16), "hid", j) for j in range(hid_count - 1, 0, -1)
    ]
    total = partial_of(0)
    for part in received:
        total = total + part.astype(f32)
    slot_box = jnp.broadcast_to(slot_part.reshape(1, -1), (8, seq_count * capacity))
    slot_all = slot_box
    for j in range(1, hid_count):
        slot_all = slot_all + swap(slot_box, "hid", j)
    own_sum = total[:capacity]
    slot_grad = slot_all[:, :capacity]
    for k in range(1, seq_count):
        lines = slice(k * capacity, (k + 1) * capacity)
        own_sum = own_sum + swap(total[lines].astype(bf16), "seq", k).astype(f32)
        slot_grad = slot_grad + swap(slot_all[:, lines], "seq", k)

    half = own_sum.astype(bf16)
    other_half = swap(half, "exp", 1)
    other_slot = swap(slot_grad, "exp", 1)
    d_tokens = jnp.dot(select_own, half, preferred_element_type=f32) + jnp.dot(
        select_other, other_half, preferred_element_type=f32
    )
    d_gates = jnp.sum(pick_own * slot_grad[0][None, None, :], axis=2) + jnp.sum(
        pick_other * other_slot[0][None, None, :], axis=2
    )

    grad_down = lax.dot_general(
        weighted, grads_e, contract_rows, preferred_element_type=f32
    ).astype(bf16)
    grad_gate = lax.dot_general(
        rows_e, d_gate, contract_rows, preferred_element_type=f32
    ).astype(bf16)
    grad_up = lax.dot_general(
        rows_e, d_up, contract_rows, preferred_element_type=f32
    ).astype(bf16)
    return (grad_gate[None], grad_up[None], grad_down[None], d_tokens, d_gates)


def solution(mesh):
    return jax.shard_map(
        on_device,
        mesh=mesh,
        in_specs=(
            P("seq", None),
            P("seq", None),
            P("seq", None),
            P("seq", None),
            P("exp", None, ("seq", "hid")),
            P("exp", None, ("seq", "hid")),
            P("exp", ("seq", "hid"), None),
        ),
        out_specs=(
            P("exp", None, ("seq", "hid")),
            P("exp", None, ("seq", "hid")),
            P("exp", ("seq", "hid"), None),
            P("seq", "hid"),
            P("seq", None),
        ),
        check_vma=False,
    )
```

```python
import functools

import jax
import jax.numpy as jnp
from jax import lax
from jax.experimental import pallas as pl
from jax.experimental.pallas import tpu as pltpu
from jax.sharding import PartitionSpec as P

LANES = 128
VMEM_LIMIT = 16 * 1024 * 1024
FETCH_PARTS = 8
LAST = (((1,), (1,)), ((), ()))
FIRST = (((0,), (0,)), ((), ()))


def swap(x, axis, bits):
    size = lax.axis_size(axis)
    return lax.ppermute(x, axis, [(i, i ^ bits) for i in range(size)])


def block_of(extent, most):
    size = most
    while extent % size:
        size -= LANES
    return size


def pick_of(expert_ids, expert, capacity):
    tok_rows = expert_ids.shape[0]
    chosen = (expert_ids == expert).astype(jnp.int32)
    slot_index = (jnp.cumsum(chosen.reshape(-1)) - 1).reshape(tok_rows, 2)
    columns = jnp.arange(capacity, dtype=jnp.int32)
    return (
        (chosen[:, :, None] == 1) & (slot_index[:, :, None] == columns[None, None, :])
    ).astype(jnp.float32)


def fetch_kernel(*refs):
    count = (len(refs) - 1) // 2
    sources, targets, sems = refs[:count], refs[count : 2 * count], refs[-1]
    copies = []
    for m in range(count):
        lines = sources[m].shape[0] // FETCH_PARTS
        for i in range(FETCH_PARTS):
            part = pl.ds(i * lines, lines)
            copies.append(
                pltpu.make_async_copy(sources[m].at[part], targets[m].at[part], sems.at[m, i])
            )
    for copy in copies:
        copy.start()
    for copy in copies:
        copy.wait()


def fetch(*arrays):
    return pl.pallas_call(
        fetch_kernel,
        in_specs=[pl.BlockSpec(memory_space=pl.ANY)] * len(arrays),
        out_specs=[pl.BlockSpec(memory_space=pltpu.VMEM)] * len(arrays),
        out_shape=[pltpu.VMEM(x.shape, x.dtype) for x in arrays],
        scratch_shapes=[pltpu.SemaphoreType.DMA((len(arrays), FETCH_PARTS))],
        compiler_params=pltpu.CompilerParams(vmem_limit_bytes=VMEM_LIMIT),
        name="fetch",
    )(*arrays)


def forward_kernel(
    rows_ref, grads_ref, gate_ref, up_ref, down_ref, hidden_ref, d_gate_ref, d_up_ref, slot_ref,
    gate_acc, up_acc, back_acc,
):
    width = rows_ref.shape[1]
    block = block_of(width, 512)

    def add(i, first):
        lines = pl.ds(pl.multiple_of(i * block, block), block)
        gate = jnp.dot(rows_ref[:, lines], gate_ref[lines, :], preferred_element_type=jnp.float32)
        up = jnp.dot(rows_ref[:, lines], up_ref[lines, :], preferred_element_type=jnp.float32)
        back = lax.dot_general(
            down_ref[:, lines], grads_ref[:, lines], LAST, preferred_element_type=jnp.float32
        )
        if first:
            gate_acc[...] = gate
            up_acc[...] = up
            back_acc[...] = back
        else:
            gate_acc[...] += gate
            up_acc[...] += up
            back_acc[...] += back

    add(0, True)

    @pl.loop(1, width // block)
    def _(i):
        add(i, False)

    back = back_acc[...].T
    gate = gate_acc[...]
    up = up_acc[...]
    sig = jax.nn.sigmoid(gate)
    activated = gate * sig
    hidden = (activated * up).astype(jnp.bfloat16)
    hidden_ref[...] = hidden
    slots = jnp.sum(hidden.astype(jnp.float32) * back, axis=1, keepdims=True)
    slot_ref[...] = jnp.broadcast_to(slots, slot_ref.shape)
    d_gate_ref[...] = (back * up * (sig * (1.0 + gate * (1.0 - sig)))).astype(jnp.bfloat16)
    d_up_ref[...] = (back * activated).astype(jnp.bfloat16)


def forward_step(rows, grads, gate_mat, up_mat, down_mat):
    count, width = rows.shape
    hidden_local = gate_mat.shape[1]
    half = jax.ShapeDtypeStruct((count, hidden_local), jnp.bfloat16)
    acc = pltpu.VMEM((count, hidden_local), jnp.float32)
    return pl.pallas_call(
        forward_kernel,
        in_specs=[pl.BlockSpec(memory_space=pltpu.VMEM)] * 5,
        out_specs=[pl.BlockSpec(memory_space=pltpu.VMEM)] * 4,
        out_shape=[half, half, half, jax.ShapeDtypeStruct((count, LANES), jnp.float32)],
        scratch_shapes=[acc, acc, pltpu.VMEM((hidden_local, count), jnp.float32)],
        compiler_params=pltpu.CompilerParams(vmem_limit_bytes=VMEM_LIMIT),
        name="forward_step",
    )(rows, grads, gate_mat, up_mat, down_mat)


def piece_kernel(piece_ref, d_gate_ref, d_up_ref, slot_ref, gate_ref, up_ref, out_ref):
    piece = out_ref.shape[1] - LANES
    block = block_of(piece, 384)
    for i in range(piece // block):
        lines = pl.ds(pl.multiple_of(piece_ref[0] * piece + i * block, LANES), block)
        part = lax.dot_general(
            gate_ref[lines, :], d_gate_ref[...], LAST, preferred_element_type=jnp.float32
        ) + lax.dot_general(up_ref[lines, :], d_up_ref[...], LAST, preferred_element_type=jnp.float32)
        out_ref[:, i * block : (i + 1) * block] = part.T.astype(out_ref.dtype)
    out_ref[:, piece:] = slot_ref[...].astype(out_ref.dtype)


def row_piece(index, d_gate, d_up, slots, gate_mat, up_mat, piece, dtype):
    rows, hidden_local = d_gate.shape
    return pl.pallas_call(
        piece_kernel,
        in_specs=[pl.BlockSpec(memory_space=pltpu.SMEM)] + [pl.BlockSpec(memory_space=pltpu.VMEM)] * 5,
        out_specs=pl.BlockSpec(memory_space=pltpu.VMEM),
        out_shape=jax.ShapeDtypeStruct((rows, piece + LANES), dtype),
        compiler_params=pltpu.CompilerParams(vmem_limit_bytes=VMEM_LIMIT),
        name="row_piece",
    )(index.reshape(1), d_gate, d_up, slots, gate_mat, up_mat)


def on_device(tokens, out_grad, expert_ids, gate_probs, w_gate, w_up, w_down):
    expert = lax.axis_index("exp")
    hid = lax.axis_index("hid")
    tok_rows, model_width = tokens.shape
    capacity = 5 * tok_rows // 16
    seq_count = lax.axis_size("seq")
    hid_count = lax.axis_size("hid")
    piece = model_width // hid_count
    bf16, f32 = jnp.bfloat16, jnp.float32

    pick_own = pick_of(expert_ids, expert, capacity)
    select_own = jnp.sum(pick_own, axis=1).astype(bf16)
    weight_own = jnp.sum(pick_own * gate_probs[:, :, None], axis=(0, 1))

    def slots_of(x):
        return lax.dot_general(select_own, x, FIRST, preferred_element_type=f32)

    def row_slots(x):
        return slots_of(x).astype(bf16)

    def grad_slots(x):
        return (slots_of(x) * weight_own[:, None]).astype(bf16)

    def quarter(x):
        return lax.dynamic_slice_in_dim(x, hid * piece, piece, axis=1)

    message = jnp.concatenate([row_slots(quarter(tokens)), grad_slots(quarter(out_grad))], axis=0)

    def after(x, done):
        return lax.optimization_barrier((x, done))[0]

    pieces = [[None] * seq_count for _ in range(hid_count)]
    for k in range(seq_count - 1, 0, -1):
        pieces[0][k] = swap(message, "seq", k)
    gate_mat, up_mat, down_mat, _ = after((w_gate[0], w_up[0], w_down[0], 0), message)
    gate_mat, up_mat, down_mat = fetch(gate_mat, up_mat, down_mat)
    pieces[0] = after(pieces[0], gate_mat[:8, :LANES])
    for k in range(seq_count - 1, 0, -1):
        block = pieces[0][k]
        if hid_count == 4:
            one, two = swap(block, "hid", 1), swap(block, "hid", 2)
            pieces[1][k], pieces[2][k] = one, two
            pieces[3][k] = jnp.concatenate(
                [swap(one[:capacity], "hid", 2), swap(two[capacity:], "hid", 1)], axis=0
            )
        else:
            for j in range(1, hid_count):
                pieces[j][k] = swap(block, "hid", j)
    row_pieces = [[x[:capacity] for x in y[1:]] for y in pieces]
    grad_pieces = [[x[capacity:] for x in y[1:]] for y in pieces]

    def whole(own, pieces):
        rest = jnp.zeros(((seq_count - 1) * capacity, model_width), bf16)
        for j in range(hid_count):
            rest = lax.dynamic_update_slice_in_dim(
                rest, jnp.concatenate(pieces[j], axis=0), (hid ^ j) * piece, axis=1
            )
        return jnp.concatenate([own, rest], axis=0)

    rows_e = whole(row_slots(tokens), row_pieces)
    grads_e = whole(grad_slots(out_grad), grad_pieces)

    hidden, d_gate, d_up, slots = forward_step(rows_e, grads_e, gate_mat, up_mat, down_mat)

    received = []
    source = (d_gate, d_up, slots)
    for j in range(hid_count - 1, -1, -1):
        part = row_piece(hid ^ j, *source, gate_mat, up_mat, piece, bf16 if j else f32)
        source = after(source, part)
        if j:
            received.append(swap(part, "hid", j))
    total = part
    hidden, d_gate, d_up = after((hidden, d_gate, d_up), part)
    for part in received:
        total = total + part.astype(f32)
    own_sum = total[:capacity]
    for k in range(1, seq_count):
        lines = slice(k * capacity, (k + 1) * capacity)
        own_sum = own_sum + swap(total[lines].astype(bf16), "seq", k).astype(f32)

    half = own_sum.astype(bf16)
    other_half = swap(half, "exp", 1)
    pick_other = pick_of(expert_ids, 1 - expert, capacity)
    select_other = jnp.sum(pick_other, axis=1).astype(bf16)
    d_tokens = jnp.dot(select_own, half[:, :piece], preferred_element_type=f32) + jnp.dot(
        select_other, other_half[:, :piece], preferred_element_type=f32
    )
    slot_own = own_sum[:, piece]
    slot_other = other_half[:, piece].astype(f32)
    d_gates = (
        jnp.sum(pick_own * slot_own[None, None, :], axis=2)
        + jnp.sum(pick_other * slot_other[None, None, :], axis=2)
    ) / gate_probs

    grad_down = lax.dot_general(hidden, grads_e, FIRST, preferred_element_type=f32).astype(bf16)
    grad_gate = lax.dot_general(rows_e, d_gate, FIRST, preferred_element_type=f32).astype(bf16)
    grad_up = lax.dot_general(rows_e, d_up, FIRST, preferred_element_type=f32).astype(bf16)
    return (grad_gate[None], grad_up[None], grad_down[None], d_tokens, d_gates)


def solution(mesh):
    return jax.shard_map(
        on_device,
        mesh=mesh,
        in_specs=(
            P("seq", None),
            P("seq", None),
            P("seq", None),
            P("seq", None),
            P("exp", None, ("seq", "hid")),
            P("exp", None, ("seq", "hid")),
            P("exp", ("seq", "hid"), None),
        ),
        out_specs=(
            P("exp", None, ("seq", "hid")),
            P("exp", None, ("seq", "hid")),
            P("exp", ("seq", "hid"), None),
            P("seq", "hid"),
            P("seq", None),
        ),
        check_vma=False,
    )
```

```python
import functools

import functools

import jax
import jax.numpy as jnp
from jax import lax
from jax.experimental import pallas as pl
from jax.experimental.pallas import tpu as pltpu
from jax.sharding import PartitionSpec as P

LANES = 128
VMEM_LIMIT = 8 * 1024 * 1024
FETCH_PARTS = 8
LAST = (((1,), (1,)), ((), ()))
FIRST = (((0,), (0,)), ((), ()))


def swap(x, axis, bits):
    size = lax.axis_size(axis)
    return lax.ppermute(x, axis, [(i, i ^ bits) for i in range(size)])


def block_of(extent, most):
    size = most
    while extent % size:
        size -= LANES
    return size


def pick_of(expert_ids, expert, capacity):
    tok_rows = expert_ids.shape[0]
    chosen = (expert_ids == expert).astype(jnp.int32)
    slot_index = (jnp.cumsum(chosen.reshape(-1)) - 1).reshape(tok_rows, 2)
    columns = jnp.arange(capacity, dtype=jnp.int32)
    return (
        (chosen[:, :, None] == 1) & (slot_index[:, :, None] == columns[None, None, :])
    ).astype(jnp.float32)


def fetch_kernel(*refs):
    count = (len(refs) - 1) // 2
    sources, targets, sems = refs[:count], refs[count : 2 * count], refs[-1]
    copies = []
    for m in range(count):
        lines = sources[m].shape[0] // FETCH_PARTS
        for i in range(FETCH_PARTS):
            part = pl.ds(i * lines, lines)
            copies.append(
                pltpu.make_async_copy(sources[m].at[part], targets[m].at[part], sems.at[m, i])
            )
    for copy in copies:
        copy.start()
    for copy in copies:
        copy.wait()


def fetch(*arrays):
    return pl.pallas_call(
        fetch_kernel,
        in_specs=[pl.BlockSpec(memory_space=pltpu.HBM)] * len(arrays),
        out_specs=[pl.BlockSpec(memory_space=pltpu.VMEM)] * len(arrays),
        out_shape=[pltpu.VMEM(x.shape, x.dtype) for x in arrays],
        scratch_shapes=[pltpu.SemaphoreType.DMA((len(arrays), FETCH_PARTS))],
        compiler_params=pltpu.CompilerParams(vmem_limit_bytes=VMEM_LIMIT),
        name="fetch",
    )(*(pltpu.with_memory_space_constraint(x, pltpu.HBM) for x in arrays))


def columns_kernel(index_ref, source_ref, *refs):
    targets, sems = refs[:-1], refs[-1]
    height, width = targets[0].shape
    lines = height // FETCH_PARTS
    copies = []
    for j, target in enumerate(targets):
        start = pl.multiple_of((index_ref[0] ^ j) * width, LANES)
        for i in range(FETCH_PARTS):
            part = pl.ds(i * lines, lines)
            copies.append(
                pltpu.make_async_copy(
                    source_ref.at[part, pl.ds(start, width)], target.at[part], sems.at[j, i]
                )
            )
    for copy in copies:
        copy.start()
    for copy in copies:
        copy.wait()


def fetch_columns(index, array, count):
    height, width = array.shape[0], array.shape[1] // count
    return pl.pallas_call(
        columns_kernel,
        in_specs=[
            pl.BlockSpec(memory_space=pltpu.SMEM),
            pl.BlockSpec(memory_space=pltpu.HBM),
        ],
        out_specs=[pl.BlockSpec(memory_space=pltpu.VMEM)] * count,
        out_shape=[pltpu.VMEM((height, width), array.dtype)] * count,
        scratch_shapes=[pltpu.SemaphoreType.DMA((count, FETCH_PARTS))],
        compiler_params=pltpu.CompilerParams(vmem_limit_bytes=VMEM_LIMIT),
        name="fetch_columns",
    )(index.reshape(1), pltpu.with_memory_space_constraint(array, pltpu.HBM))


def pair_kernel(first, index_ref, rows_ref, gate_ref, up_ref, *refs):
    piece = rows_ref.shape[1]
    block = block_of(piece, 512)
    gate_out, up_out = refs[-2:]
    gate, up = (None, None) if first else (refs[0][...], refs[1][...])
    for i in range(piece // block):
        lines = pl.ds(pl.multiple_of(index_ref[0] * piece + i * block, LANES), block)
        rows = rows_ref[:, i * block : (i + 1) * block]
        more_gate = jnp.dot(rows, gate_ref[lines, :], preferred_element_type=jnp.float32)
        more_up = jnp.dot(rows, up_ref[lines, :], preferred_element_type=jnp.float32)
        gate = more_gate if gate is None else gate + more_gate
        up = more_up if up is None else up + more_up
    gate_out[...] = gate
    up_out[...] = up


def back_kernel(first, last, grads_ref, down_ref, *refs):
    piece = grads_ref.shape[1]
    block = block_of(piece, 512)
    back = None if first else refs[0][...]
    for i in range(piece // block):
        lines = slice(i * block, (i + 1) * block)
        grads = grads_ref[:, lines]
        more = lax.dot_general(
            down_ref[:, lines], grads, LAST, preferred_element_type=jnp.float32
        )
        back = more if back is None else back + more
    if not last:
        refs[-1][...] = back
        return
    gate_ref, up_ref, hidden_ref, d_gate_ref, d_up_ref, slot_ref = refs[-6:]
    back = back.T
    gate = gate_ref[...]
    up = up_ref[...]
    sig = jax.nn.sigmoid(gate)
    activated = gate * sig
    hidden = (activated * up).astype(jnp.bfloat16)
    hidden_ref[...] = hidden
    slots = jnp.sum(hidden.astype(jnp.float32) * back, axis=1, keepdims=True)
    slot_ref[...] = jnp.broadcast_to(slots, slot_ref.shape)
    d_gate_ref[...] = (back * up * (sig * (1.0 + gate * (1.0 - sig)))).astype(jnp.bfloat16)
    d_up_ref[...] = (back * activated).astype(jnp.bfloat16)


def whole_call(kernel, name, outs, index, *arrays):
    scalars = [] if index is None else [index.reshape(1)]
    return pl.pallas_call(
        kernel,
        in_specs=[pl.BlockSpec(memory_space=pltpu.SMEM)] * len(scalars)
        + [pl.BlockSpec(memory_space=pltpu.VMEM)] * len(arrays),
        out_specs=[pl.BlockSpec(memory_space=pltpu.VMEM)] * len(outs),
        out_shape=[jax.ShapeDtypeStruct(*x) for x in outs],
        compiler_params=pltpu.CompilerParams(vmem_limit_bytes=VMEM_LIMIT),
        name=name,
    )(*scalars, *arrays)


def pair_step(index, rows, gate_mat, up_mat, acc):
    shape = ((rows.shape[0], gate_mat.shape[1]), jnp.float32)
    kernel = functools.partial(pair_kernel, not acc)
    return whole_call(kernel, "pair_step", [shape, shape], index, rows, gate_mat, up_mat, *acc)


def back_step(grads, down_mat, acc, last):
    rows, hidden_local = grads.shape[0], down_mat.shape[0]
    half = ((rows, hidden_local), jnp.bfloat16)
    if last:
        outs = [half, half, half, ((rows, LANES), jnp.float32)]
    else:
        outs = [((hidden_local, rows), jnp.float32)]
    kernel = functools.partial(back_kernel, not acc, bool(last))
    return whole_call(kernel, "back_step", outs, None, grads, down_mat, *acc, *last)


def piece_kernel(piece_ref, d_gate_ref, d_up_ref, slot_ref, gate_ref, up_ref, out_ref):
    piece = out_ref.shape[1] - LANES
    block = block_of(piece, 384)
    for i in range(piece // block):
        lines = pl.ds(pl.multiple_of(piece_ref[0] * piece + i * block, LANES), block)
        part = lax.dot_general(
            gate_ref[lines, :], d_gate_ref[...], LAST, preferred_element_type=jnp.float32
        ) + lax.dot_general(up_ref[lines, :], d_up_ref[...], LAST, preferred_element_type=jnp.float32)
        out_ref[:, i * block : (i + 1) * block] = part.T.astype(out_ref.dtype)
    out_ref[:, piece:] = slot_ref[...].astype(out_ref.dtype)


def row_piece(index, d_gate, d_up, slots, gate_mat, up_mat, piece, dtype):
    rows, hidden_local = d_gate.shape
    return pl.pallas_call(
        piece_kernel,
        in_specs=[pl.BlockSpec(memory_space=pltpu.SMEM)] + [pl.BlockSpec(memory_space=pltpu.VMEM)] * 5,
        out_specs=pl.BlockSpec(memory_space=pltpu.VMEM),
        out_shape=jax.ShapeDtypeStruct((rows, piece + LANES), dtype),
        compiler_params=pltpu.CompilerParams(vmem_limit_bytes=VMEM_LIMIT),
        name="row_piece",
    )(index.reshape(1), d_gate, d_up, slots, gate_mat, up_mat)


def on_device(tokens, out_grad, expert_ids, gate_probs, w_gate, w_up, w_down):
    expert = lax.axis_index("exp")
    hid = lax.axis_index("hid")
    tok_rows, model_width = tokens.shape
    capacity = 5 * tok_rows // 16
    seq_count = lax.axis_size("seq")
    hid_count = lax.axis_size("hid")
    piece = model_width // hid_count
    bf16, f32 = jnp.bfloat16, jnp.float32

    pick_own = pick_of(expert_ids, expert, capacity)
    select_own = jnp.sum(pick_own, axis=1).astype(bf16)
    weight_own = jnp.sum(pick_own * gate_probs[:, :, None], axis=(0, 1))

    def slots_of(x):
        return lax.dot_general(select_own, x, FIRST, preferred_element_type=f32)

    def row_slots(x):
        return slots_of(x).astype(bf16)

    def grad_slots(x):
        return (slots_of(x) * weight_own[:, None]).astype(bf16)

    def quarter(x):
        return lax.dynamic_slice_in_dim(x, hid * piece, piece, axis=1)

    def after(x, done):
        return lax.optimization_barrier((x, done))[0]

    def spread(x):
        return [swap(x, "seq", k) for k in range(1, seq_count)]

    def across(x):
        return [swap(x, "hid", j) for j in ((1, 2) if hid_count == 4 else range(1, hid_count))]

    remote = (seq_count - 1) * capacity
    split = -(-remote // 32) * 16

    def corner(one, two):
        if hid_count != 4:
            return []
        return [
            jnp.concatenate([swap(one[:split], "hid", 2), swap(two[split:], "hid", 1)], axis=0)
        ]

    def with_own(own, x, j):
        mine = lax.dynamic_slice_in_dim(own, (hid ^ j) * piece, piece, axis=1)
        return jnp.concatenate([mine, x], axis=0)

    row_message = row_slots(quarter(tokens))
    row_blocks = spread(row_message)
    grad_message = after(grad_slots(quarter(out_grad)), row_message)
    grad_blocks = spread(grad_message)
    own_rows = row_slots(tokens)
    own_grads = grad_slots(out_grad)
    gate_mat, up_mat = after((w_gate[0], w_up[0]), (grad_message, own_rows, own_grads))
    gate_mat, up_mat = fetch(gate_mat, up_mat)
    row_blocks = after(row_blocks, gate_mat[:8, :LANES])
    row_parts = [jnp.concatenate(row_blocks, axis=0)]
    row_across = across(row_parts[0])
    down = fetch_columns(hid, after(w_down[0], row_parts[0]), hid_count)
    pair = pair_step(
        hid, with_own(own_rows, row_parts[0], 0), gate_mat, up_mat, ()
    )
    grad_blocks = after(grad_blocks, (pair, down[0][:8, :LANES]))
    grad_parts = [jnp.concatenate(grad_blocks, axis=0)]
    grad_across = across(grad_parts[0])
    row_across = after(row_across, grad_parts[0])
    row_corner = corner(row_across[0], row_across[1])
    for j, x in enumerate(row_across, 1):
        pair = pair_step(hid ^ j, with_own(own_rows, x, j), gate_mat, up_mat, pair)
    grad_across = after(grad_across, pair)
    grad_corner = corner(grad_across[0], grad_across[1])
    row_corner = after(row_corner, grad_across)
    for j, x in enumerate(row_corner, 3):
        pair = pair_step(hid ^ j, with_own(own_rows, x, j), gate_mat, up_mat, pair)
    back = back_step(with_own(own_grads, grad_parts[0], 0), down[0], (), ())
    rest = list(enumerate(grad_across, 1))
    if not grad_corner:
        final = rest.pop()
    for j, x in rest:
        back = back_step(with_own(own_grads, x, j), down[j], back, ())
    if grad_corner:
        final = (3, after(grad_corner[0], (back, pair)))
    row_parts += row_across + row_corner
    grad_parts += grad_across + grad_corner
    j, x = final
    hidden, d_gate, d_up, slots = back_step(
        with_own(own_grads, x, j), down[j], back, pair
    )

    def whole(own, parts):
        rest = jnp.zeros((remote, model_width), bf16)
        for j in range(hid_count):
            rest = lax.dynamic_update_slice_in_dim(rest, parts[j], (hid ^ j) * piece, axis=1)
        return jnp.concatenate([own, rest], axis=0)

    received = []
    source = (d_gate, d_up, slots)
    for j in range(hid_count - 1, -1, -1):
        part = row_piece(hid ^ j, *source, gate_mat, up_mat, piece, bf16 if j else f32)
        source = after(source, part)
        if j:
            received.append(swap(part, "hid", j))
    total = part
    hidden, d_gate, d_up = after((hidden, d_gate, d_up), part)
    rows_e = whole(own_rows, after(row_parts, part))
    grads_e = whole(own_grads, after(grad_parts, part))
    for part in received:
        total = total + part.astype(f32)
    own_sum = total[:capacity]
    for k in range(1, seq_count):
        lines = slice(k * capacity, (k + 1) * capacity)
        own_sum = own_sum + swap(total[lines].astype(bf16), "seq", k).astype(f32)

    half = own_sum.astype(bf16)
    other_half = swap(half, "exp", 1)
    pick_other = pick_of(expert_ids, 1 - expert, capacity)
    select_other = jnp.sum(pick_other, axis=1).astype(bf16)
    d_tokens = jnp.dot(select_own, half[:, :piece], preferred_element_type=f32) + jnp.dot(
        select_other, other_half[:, :piece], preferred_element_type=f32
    )
    slot_own = own_sum[:, piece]
    slot_other = other_half[:, piece].astype(f32)
    d_gates = (
        jnp.sum(pick_own * slot_own[None, None, :], axis=2)
        + jnp.sum(pick_other * slot_other[None, None, :], axis=2)
    ) / gate_probs

    grad_down = lax.dot_general(hidden, grads_e, FIRST, preferred_element_type=f32).astype(bf16)
    grad_gate = lax.dot_general(rows_e, d_gate, FIRST, preferred_element_type=f32).astype(bf16)
    grad_up = lax.dot_general(rows_e, d_up, FIRST, preferred_element_type=f32).astype(bf16)
    return (grad_gate[None], grad_up[None], grad_down[None], d_tokens, d_gates)


def solution(mesh):
    return jax.shard_map(
        on_device,
        mesh=mesh,
        in_specs=(
            P("seq", None),
            P("seq", None),
            P("seq", None),
            P("seq", None),
            P("exp", None, ("seq", "hid")),
            P("exp", None, ("seq", "hid")),
            P("exp", ("seq", "hid"), None),
        ),
        out_specs=(
            P("exp", None, ("seq", "hid")),
            P("exp", None, ("seq", "hid")),
            P("exp", ("seq", "hid"), None),
            P("seq", "hid"),
            P("seq", None),
        ),
        check_vma=False,
    )
```

```python
import functools

import functools

import jax
import jax.numpy as jnp
from jax import lax
from jax.experimental import pallas as pl
from jax.experimental.pallas import tpu as pltpu
from jax.sharding import PartitionSpec as P

LANES = 128
VMEM_LIMIT = 8 * 1024 * 1024
FETCH_PARTS = 8
LAST = (((1,), (1,)), ((), ()))
FIRST = (((0,), (0,)), ((), ()))


def swap(x, axis, bits):
    size = lax.axis_size(axis)
    return lax.ppermute(x, axis, [(i, i ^ bits) for i in range(size)])


def block_of(extent, most):
    size = most
    while extent % size:
        size -= LANES
    return size


def pick_of(expert_ids, expert, capacity):
    tok_rows = expert_ids.shape[0]
    chosen = (expert_ids == expert).astype(jnp.int32)
    slot_index = (jnp.cumsum(chosen.reshape(-1)) - 1).reshape(tok_rows, 2)
    columns = jnp.arange(capacity, dtype=jnp.int32)
    return (
        (chosen[:, :, None] == 1) & (slot_index[:, :, None] == columns[None, None, :])
    ).astype(jnp.float32)


def place_kernel(
    expert_ref, ids_ref, probs_ref, own_ref, other_ref, half_ref, other_half_ref,
    tokens_ref, gates_ref,
):
    piece = tokens_ref.shape[1]
    own, other = own_ref[...], other_ref[...]
    half, other_half = half_ref[...], other_half_ref[...]
    tokens_ref[...] = jnp.dot(own, half[:, :piece], preferred_element_type=jnp.float32) + jnp.dot(
        other, other_half[:, :piece], preferred_element_type=jnp.float32
    )
    ids = ids_ref[...]

    def gates(select, sums, expert):
        token = lax.dot_general(
            sums[:, piece:], select, (((0,), (1,)), ((), ())), preferred_element_type=jnp.float32
        )
        return jnp.where(ids == expert, token[:1], 0.0)

    mine = expert_ref[0]
    gates_ref[...] = (gates(own, half, mine) + gates(other, other_half, 1 - mine)) / probs_ref[...]


def sum_kernel(own_ref, *refs):
    capacity = refs[-1].shape[0]
    first = len(refs) - own_ref.shape[0] // capacity
    parts, outs = refs[:first], refs[first:]
    for k, out in enumerate(outs):
        lines = slice(k * capacity, (k + 1) * capacity)
        total = own_ref[lines, :]
        for part in parts:
            total = total + part[lines, :].astype(jnp.float32)
        out[...] = total.astype(out.dtype)


def fetch_kernel(*refs):
    count = (len(refs) - 1) // 2
    sources, targets, sems = refs[:count], refs[count : 2 * count], refs[-1]
    copies = []
    for m in range(count):
        lines = sources[m].shape[0] // FETCH_PARTS
        for i in range(FETCH_PARTS):
            part = pl.ds(i * lines, lines)
            copies.append(
                pltpu.make_async_copy(sources[m].at[part], targets[m].at[part], sems.at[m, i])
            )
    for copy in copies:
        copy.start()
    for copy in copies:
        copy.wait()


def fetch(*arrays):
    return pl.pallas_call(
        fetch_kernel,
        in_specs=[pl.BlockSpec(memory_space=pltpu.HBM)] * len(arrays),
        out_specs=[pl.BlockSpec(memory_space=pltpu.VMEM)] * len(arrays),
        out_shape=[pltpu.VMEM(x.shape, x.dtype) for x in arrays],
        scratch_shapes=[pltpu.SemaphoreType.DMA((len(arrays), FETCH_PARTS))],
        compiler_params=pltpu.CompilerParams(vmem_limit_bytes=VMEM_LIMIT),
        name="fetch",
    )(*(pltpu.with_memory_space_constraint(x, pltpu.HBM) for x in arrays))


def columns_kernel(index_ref, source_ref, *refs):
    targets, sems = refs[:-1], refs[-1]
    height, width = targets[0].shape
    lines = height // FETCH_PARTS
    copies = []
    for j, target in enumerate(targets):
        start = pl.multiple_of((index_ref[0] ^ j) * width, LANES)
        for i in range(FETCH_PARTS):
            part = pl.ds(i * lines, lines)
            copies.append(
                pltpu.make_async_copy(
                    source_ref.at[part, pl.ds(start, width)], target.at[part], sems.at[j, i]
                )
            )
    for copy in copies:
        copy.start()
    for copy in copies:
        copy.wait()


def fetch_columns(index, array, count):
    height, width = array.shape[0], array.shape[1] // count
    return pl.pallas_call(
        columns_kernel,
        in_specs=[
            pl.BlockSpec(memory_space=pltpu.SMEM),
            pl.BlockSpec(memory_space=pltpu.HBM),
        ],
        out_specs=[pl.BlockSpec(memory_space=pltpu.VMEM)] * count,
        out_shape=[pltpu.VMEM((height, width), array.dtype)] * count,
        scratch_shapes=[pltpu.SemaphoreType.DMA((count, FETCH_PARTS))],
        compiler_params=pltpu.CompilerParams(vmem_limit_bytes=VMEM_LIMIT),
        name="fetch_columns",
    )(index.reshape(1), pltpu.with_memory_space_constraint(array, pltpu.HBM))


def pair_kernel(first, index_ref, rows_ref, gate_ref, up_ref, *refs):
    piece = rows_ref.shape[1]
    block = block_of(piece, 512)
    gate_out, up_out = refs[-2:]
    gate, up = (None, None) if first else (refs[0][...], refs[1][...])
    for i in range(piece // block):
        lines = pl.ds(pl.multiple_of(index_ref[0] * piece + i * block, LANES), block)
        rows = rows_ref[:, i * block : (i + 1) * block]
        more_gate = jnp.dot(rows, gate_ref[lines, :], preferred_element_type=jnp.float32)
        more_up = jnp.dot(rows, up_ref[lines, :], preferred_element_type=jnp.float32)
        gate = more_gate if gate is None else gate + more_gate
        up = more_up if up is None else up + more_up
    gate_out[...] = gate
    up_out[...] = up


def back_kernel(first, last, grads_ref, down_ref, *refs):
    piece = grads_ref.shape[1]
    block = block_of(piece, 512)
    back = None if first else refs[0][...]
    for i in range(piece // block):
        lines = slice(i * block, (i + 1) * block)
        grads = grads_ref[:, lines]
        more = lax.dot_general(
            down_ref[:, lines], grads, LAST, preferred_element_type=jnp.float32
        )
        back = more if back is None else back + more
    if not last:
        refs[-1][...] = back
        return
    gate_ref, up_ref, hidden_ref, d_gate_ref, d_up_ref, slot_ref = refs[-6:]
    back = back.T
    gate = gate_ref[...]
    up = up_ref[...]
    sig = jax.nn.sigmoid(gate)
    activated = gate * sig
    hidden = (activated * up).astype(jnp.bfloat16)
    hidden_ref[...] = hidden
    slots = jnp.sum(hidden.astype(jnp.float32) * back, axis=1, keepdims=True)
    slot_ref[...] = jnp.broadcast_to(slots, slot_ref.shape)
    d_gate_ref[...] = (back * up * (sig * (1.0 + gate * (1.0 - sig)))).astype(jnp.bfloat16)
    d_up_ref[...] = (back * activated).astype(jnp.bfloat16)


def whole_call(kernel, name, outs, index, *arrays):
    scalars = [] if index is None else [index.reshape(1)]
    return pl.pallas_call(
        kernel,
        in_specs=[pl.BlockSpec(memory_space=pltpu.SMEM)] * len(scalars)
        + [pl.BlockSpec(memory_space=pltpu.VMEM)] * len(arrays),
        out_specs=[pl.BlockSpec(memory_space=pltpu.VMEM)] * len(outs),
        out_shape=[jax.ShapeDtypeStruct(*x) for x in outs],
        compiler_params=pltpu.CompilerParams(vmem_limit_bytes=VMEM_LIMIT),
        name=name,
    )(*scalars, *arrays)


def pair_step(index, rows, gate_mat, up_mat, acc):
    shape = ((rows.shape[0], gate_mat.shape[1]), jnp.float32)
    kernel = functools.partial(pair_kernel, not acc)
    return whole_call(kernel, "pair_step", [shape, shape], index, rows, gate_mat, up_mat, *acc)


def back_step(grads, down_mat, acc, last):
    rows, hidden_local = grads.shape[0], down_mat.shape[0]
    half = ((rows, hidden_local), jnp.bfloat16)
    if last:
        outs = [half, half, half, ((rows, LANES), jnp.float32)]
    else:
        outs = [((hidden_local, rows), jnp.float32)]
    kernel = functools.partial(back_kernel, not acc, bool(last))
    return whole_call(kernel, "back_step", outs, None, grads, down_mat, *acc, *last)


def piece_kernel(piece_ref, d_gate_ref, d_up_ref, slot_ref, gate_ref, up_ref, out_ref):
    piece = out_ref.shape[1] - LANES
    block = block_of(piece, 384)
    for i in range(piece // block):
        lines = pl.ds(pl.multiple_of(piece_ref[0] * piece + i * block, LANES), block)
        part = lax.dot_general(
            gate_ref[lines, :], d_gate_ref[...], LAST, preferred_element_type=jnp.float32
        ) + lax.dot_general(up_ref[lines, :], d_up_ref[...], LAST, preferred_element_type=jnp.float32)
        out_ref[:, i * block : (i + 1) * block] = part.T.astype(out_ref.dtype)
    out_ref[:, piece:] = slot_ref[...].astype(out_ref.dtype)


def row_piece(index, d_gate, d_up, slots, gate_mat, up_mat, piece, dtype):
    rows, hidden_local = d_gate.shape
    return pl.pallas_call(
        piece_kernel,
        in_specs=[pl.BlockSpec(memory_space=pltpu.SMEM)] + [pl.BlockSpec(memory_space=pltpu.VMEM)] * 5,
        out_specs=pl.BlockSpec(memory_space=pltpu.VMEM),
        out_shape=jax.ShapeDtypeStruct((rows, piece + LANES), dtype),
        compiler_params=pltpu.CompilerParams(vmem_limit_bytes=VMEM_LIMIT),
        cost_estimate=pl.CostEstimate(
            flops=4 * rows * hidden_local * piece,
            transcendentals=0,
            bytes_accessed=4 * hidden_local * (piece + rows),
        ),
        name="row_piece",
    )(index.reshape(1), d_gate, d_up, slots, gate_mat, up_mat)


def on_device(tokens, out_grad, expert_ids, gate_probs, w_gate, w_up, w_down):
    expert = lax.axis_index("exp")
    hid = lax.axis_index("hid")
    tok_rows, model_width = tokens.shape
    capacity = 5 * tok_rows // 16
    seq_count = lax.axis_size("seq")
    hid_count = lax.axis_size("hid")
    piece = model_width // hid_count
    bf16, f32 = jnp.bfloat16, jnp.float32

    pick_own = pick_of(expert_ids, expert, capacity)
    select_own = jnp.sum(pick_own, axis=1).astype(bf16)
    weight_own = jnp.sum(pick_own * gate_probs[:, :, None], axis=(0, 1))

    def slots_of(x):
        return lax.dot_general(select_own, x, FIRST, preferred_element_type=f32)

    def row_slots(x):
        return slots_of(x).astype(bf16)

    def grad_slots(x):
        return (slots_of(x) * weight_own[:, None]).astype(bf16)

    def quarter(x):
        return lax.dynamic_slice_in_dim(x, hid * piece, piece, axis=1)

    def after(x, done):
        return lax.optimization_barrier((x, done))[0]

    def spread(x):
        return [swap(x, "seq", k) for k in range(1, seq_count)]

    def across(x):
        return [swap(x, "hid", j) for j in ((1, 2) if hid_count == 4 else range(1, hid_count))]

    remote = (seq_count - 1) * capacity
    split = -(-remote // 32) * 16

    def corner(one, two):
        if hid_count != 4:
            return []
        return [
            jnp.concatenate([swap(one[:split], "hid", 2), swap(two[split:], "hid", 1)], axis=0)
        ]

    def with_own(own, x, j):
        mine = lax.dynamic_slice_in_dim(own, (hid ^ j) * piece, piece, axis=1)
        return jnp.concatenate([mine, x], axis=0)

    row_message = row_slots(quarter(tokens))
    grad_message = after(grad_slots(quarter(out_grad)), row_message)
    own_rows, own_grads = after((row_slots(tokens), grad_slots(out_grad)), grad_message)
    gate_mat, up_mat, down_mat = w_gate[0], w_up[0], w_down[0]
    if seq_count == 4:
        row_two, row_one = swap(row_message, "seq", 2), swap(row_message, "seq", 1)
        grad_two, grad_one = swap(grad_message, "seq", 2), swap(grad_message, "seq", 1)
        row_two = after(row_two, (own_rows, own_grads))
        row_three = swap(row_two, "seq", 1)
        (gate_mat,) = fetch(after(gate_mat, row_two))
        grad_two = after(grad_two, gate_mat[:8, :LANES])
        grad_three = swap(grad_two, "seq", 1)
        row_blocks = after([row_one, row_two, row_three], grad_two)
        grad_blocks = [grad_one, grad_two, grad_three]
    else:
        row_blocks, grad_blocks = spread(row_message), spread(grad_message)
        (gate_mat,) = fetch(after(gate_mat, (own_rows, own_grads)))
        row_blocks = after(row_blocks, gate_mat[:8, :LANES])
    row_parts = [jnp.concatenate(row_blocks, axis=0)]
    row_across = across(row_parts[0])
    (up_mat,) = fetch(after(up_mat, row_parts[0]))
    grad_blocks = after(grad_blocks, up_mat[:8, :LANES])
    grad_parts = [jnp.concatenate(grad_blocks, axis=0)]
    grad_across = across(grad_parts[0])
    down = fetch_columns(hid, after(down_mat, grad_parts[0]), hid_count)
    pair = pair_step(
        hid, with_own(own_rows, after(row_parts[0], grad_parts[0]), 0), gate_mat, up_mat, ()
    )
    row_across = after(row_across, (grad_parts[0], pair, down[0][:8, :LANES]))
    row_corner = corner(row_across[0], row_across[1])
    for j, x in enumerate(row_across, 1):
        pair = pair_step(hid ^ j, with_own(own_rows, x, j), gate_mat, up_mat, pair)
    grad_across = after(grad_across, pair)
    grad_corner = corner(grad_across[0], grad_across[1])
    row_corner = after(row_corner, grad_across)
    for j, x in enumerate(row_corner, 3):
        pair = pair_step(hid ^ j, with_own(own_rows, x, j), gate_mat, up_mat, pair)
    back = back_step(with_own(own_grads, grad_parts[0], 0), down[0], (), ())
    rest = list(enumerate(grad_across, 1))
    if not grad_corner:
        final = rest.pop()
    for j, x in rest:
        back = back_step(with_own(own_grads, x, j), down[j], back, ())
    if grad_corner:
        final = (3, after(grad_corner[0], (back, pair)))
    row_parts += row_across + row_corner
    grad_parts += grad_across + grad_corner
    j, x = final
    hidden, d_gate, d_up, slots = back_step(
        with_own(own_grads, x, j), down[j], back, pair
    )

    def whole(own, parts):
        rest = jnp.zeros((remote, model_width), bf16)
        for j in range(hid_count):
            rest = lax.dynamic_update_slice_in_dim(rest, parts[j], (hid ^ j) * piece, axis=1)
        return jnp.concatenate([own, rest], axis=0)

    received = []
    source = (d_gate, d_up, slots)
    for j in range(hid_count - 1, -1, -1):
        part = row_piece(hid ^ j, *source, gate_mat, up_mat, piece, bf16 if j else f32)
        source = after(source, part)
        if j:
            received.append(swap(part, "hid", j))
    hidden, d_gate, d_up = after((hidden, d_gate, d_up), part)
    rows_e = whole(own_rows, after(row_parts, part))
    grads_e = whole(own_grads, after(grad_parts, part))
    grad_gate = lax.dot_general(rows_e, d_gate, FIRST, preferred_element_type=f32).astype(bf16)
    grad_up = lax.dot_general(rows_e, d_up, FIRST, preferred_element_type=f32).astype(bf16)
    if len(received) == 3:
        part = part + received[0].astype(f32)
        received = after(received[1:], part)
    received = after(received, (grad_gate, grad_up))
    block = (capacity, piece + LANES)
    own_sum, *messages = whole_call(
        sum_kernel, "sum_step", [(block, f32)] + [(block, bf16)] * (seq_count - 1), None, part, *received
    )
    grad_down = lax.dot_general(hidden, grads_e, FIRST, preferred_element_type=f32).astype(bf16)
    arrived = [swap(message, "seq", k) for k, message in enumerate(messages, 1)]
    for part in after(arrived, grad_down):
        own_sum = own_sum + part.astype(f32)

    half = own_sum.astype(bf16)
    other_half = swap(half, "exp", 1)
    pick_other = pick_of(expert_ids, 1 - expert, capacity)
    select_other = jnp.sum(pick_other, axis=1).astype(bf16)
    d_tokens, d_gates = whole_call(
        place_kernel,
        "place_step",
        [((tok_rows, piece), f32), ((2, tok_rows), f32)],
        expert,
        expert_ids.T,
        gate_probs.T,
        select_own,
        select_other,
        half,
        other_half,
    )

    return (grad_gate[None], grad_up[None], grad_down[None], d_tokens, d_gates.T)


def solution(mesh):
    return jax.shard_map(
        on_device,
        mesh=mesh,
        in_specs=(
            P("seq", None),
            P("seq", None),
            P("seq", None),
            P("seq", None),
            P("exp", None, ("seq", "hid")),
            P("exp", None, ("seq", "hid")),
            P("exp", ("seq", "hid"), None),
        ),
        out_specs=(
            P("exp", None, ("seq", "hid")),
            P("exp", None, ("seq", "hid")),
            P("exp", ("seq", "hid"), None),
            P("seq", "hid"),
            P("seq", None),
        ),
        check_vma=False,
    )
```

```python
import functools

import functools

import jax
import jax.numpy as jnp
from jax import lax
from jax.experimental import pallas as pl
from jax.experimental.pallas import tpu as pltpu
from jax.sharding import PartitionSpec as P

LANES = 128
VMEM_LIMIT = 8 * 1024 * 1024
FETCH_PARTS = 8
LAST = (((1,), (1,)), ((), ()))
FIRST = (((0,), (0,)), ((), ()))


def swap(x, axis, bits):
    size = lax.axis_size(axis)
    return lax.ppermute(x, axis, [(i, i ^ bits) for i in range(size)])


def block_of(extent, most):
    size = most
    while extent % size:
        size -= LANES
    return size


def pick_of(chosen, capacity):
    named = jnp.sum(chosen, axis=1)
    place = jnp.arange(chosen.shape[0], dtype=jnp.int32)
    slot = jnp.sum(jnp.where(place[None, :] < place[:, None], named[None, :], 0), axis=1)
    columns = jnp.arange(capacity, dtype=jnp.int32)
    return (named[:, None] > 0) & (slot[:, None] == columns[None, :])


def place_kernel(
    expert_ref, ids_ref, probs_ref, own_ref, other_ref, half_ref, other_half_ref,
    tokens_ref, gates_ref,
):
    piece = tokens_ref.shape[1]
    own, other = own_ref[...], other_ref[...]
    half, other_half = half_ref[...], other_half_ref[...]
    tokens_ref[...] = jnp.dot(own, half[:, :piece], preferred_element_type=jnp.float32) + jnp.dot(
        other, other_half[:, :piece], preferred_element_type=jnp.float32
    )
    ids = ids_ref[...]

    def gates(select, sums, expert):
        token = lax.dot_general(
            sums[:, piece:], select, (((0,), (1,)), ((), ())), preferred_element_type=jnp.float32
        )
        return jnp.where(ids == expert, token[:1], 0.0)

    mine = expert_ref[0]
    gates_ref[...] = (gates(own, half, mine) + gates(other, other_half, 1 - mine)) / probs_ref[...]


def sum_kernel(own_ref, *refs):
    capacity = refs[-1].shape[0]
    first = len(refs) - own_ref.shape[0] // capacity
    parts, outs = refs[:first], refs[first:]
    for k, out in enumerate(outs):
        lines = slice(k * capacity, (k + 1) * capacity)
        total = own_ref[lines, :]
        for part in parts:
            total = total + part[lines, :].astype(jnp.float32)
        out[...] = total.astype(out.dtype)


def fetch_kernel(*refs):
    count = (len(refs) - 1) // 2
    sources, targets, sems = refs[:count], refs[count : 2 * count], refs[-1]
    copies = []
    for m in range(count):
        lines = sources[m].shape[0] // FETCH_PARTS
        for i in range(FETCH_PARTS):
            part = pl.ds(i * lines, lines)
            copies.append(
                pltpu.make_async_copy(sources[m].at[part], targets[m].at[part], sems.at[m, i])
            )
    for copy in copies:
        copy.start()
    for copy in copies:
        copy.wait()


def fetch(*arrays):
    return pl.pallas_call(
        fetch_kernel,
        in_specs=[pl.BlockSpec(memory_space=pltpu.HBM)] * len(arrays),
        out_specs=[pl.BlockSpec(memory_space=pltpu.VMEM)] * len(arrays),
        out_shape=[pltpu.VMEM(x.shape, x.dtype) for x in arrays],
        scratch_shapes=[pltpu.SemaphoreType.DMA((len(arrays), FETCH_PARTS))],
        compiler_params=pltpu.CompilerParams(vmem_limit_bytes=VMEM_LIMIT),
        name="fetch",
    )(*(pltpu.with_memory_space_constraint(x, pltpu.HBM) for x in arrays))


def columns_kernel(index_ref, source_ref, *refs):
    targets, sems = refs[:-1], refs[-1]
    height, width = targets[0].shape
    lines = height // FETCH_PARTS
    copies = []
    for j, target in enumerate(targets):
        start = pl.multiple_of((index_ref[0] ^ j) * width, LANES)
        for i in range(FETCH_PARTS):
            part = pl.ds(i * lines, lines)
            copies.append(
                pltpu.make_async_copy(
                    source_ref.at[part, pl.ds(start, width)], target.at[part], sems.at[j, i]
                )
            )
    for copy in copies:
        copy.start()
    for copy in copies:
        copy.wait()


def fetch_columns(index, array, count):
    height, width = array.shape[0], array.shape[1] // count
    return pl.pallas_call(
        columns_kernel,
        in_specs=[
            pl.BlockSpec(memory_space=pltpu.SMEM),
            pl.BlockSpec(memory_space=pltpu.HBM),
        ],
        out_specs=[pl.BlockSpec(memory_space=pltpu.VMEM)] * count,
        out_shape=[pltpu.VMEM((height, width), array.dtype)] * count,
        scratch_shapes=[pltpu.SemaphoreType.DMA((count, FETCH_PARTS))],
        compiler_params=pltpu.CompilerParams(vmem_limit_bytes=VMEM_LIMIT),
        name="fetch_columns",
    )(index.reshape(1), pltpu.with_memory_space_constraint(array, pltpu.HBM))


def pair_kernel(first, index_ref, rows_ref, gate_ref, up_ref, *refs):
    piece = rows_ref.shape[1]
    block = block_of(piece, 512)
    gate_out, up_out = refs[-2:]
    gate, up = (None, None) if first else (refs[0][...], refs[1][...])
    for i in range(piece // block):
        lines = pl.ds(pl.multiple_of(index_ref[0] * piece + i * block, LANES), block)
        rows = rows_ref[:, i * block : (i + 1) * block]
        more_gate = jnp.dot(rows, gate_ref[lines, :], preferred_element_type=jnp.float32)
        more_up = jnp.dot(rows, up_ref[lines, :], preferred_element_type=jnp.float32)
        gate = more_gate if gate is None else gate + more_gate
        up = more_up if up is None else up + more_up
    gate_out[...] = gate
    up_out[...] = up


def back_kernel(first, last, grads_ref, down_ref, *refs):
    piece = grads_ref.shape[1]
    block = block_of(piece, 512)
    back = None if first else refs[0][...]
    for i in range(piece // block):
        lines = slice(i * block, (i + 1) * block)
        grads = grads_ref[:, lines]
        more = lax.dot_general(
            down_ref[:, lines], grads, LAST, preferred_element_type=jnp.float32
        )
        back = more if back is None else back + more
    if not last:
        refs[-1][...] = back
        return
    gate_ref, up_ref, hidden_ref, d_gate_ref, d_up_ref, slot_ref = refs[-6:]
    back = back.T
    gate = gate_ref[...]
    up = up_ref[...]
    sig = jax.nn.sigmoid(gate)
    activated = gate * sig
    hidden = (activated * up).astype(jnp.bfloat16)
    hidden_ref[...] = hidden
    slots = jnp.sum(hidden.astype(jnp.float32) * back, axis=1, keepdims=True)
    slot_ref[...] = jnp.broadcast_to(slots, slot_ref.shape)
    d_gate_ref[...] = (back * up * (sig * (1.0 + gate * (1.0 - sig)))).astype(jnp.bfloat16)
    d_up_ref[...] = (back * activated).astype(jnp.bfloat16)


def whole_call(kernel, name, outs, index, *arrays):
    scalars = [] if index is None else [index.reshape(1)]
    return pl.pallas_call(
        kernel,
        in_specs=[pl.BlockSpec(memory_space=pltpu.SMEM)] * len(scalars)
        + [pl.BlockSpec(memory_space=pltpu.VMEM)] * len(arrays),
        out_specs=[pl.BlockSpec(memory_space=pltpu.VMEM)] * len(outs),
        out_shape=[jax.ShapeDtypeStruct(*x) for x in outs],
        compiler_params=pltpu.CompilerParams(vmem_limit_bytes=VMEM_LIMIT),
        name=name,
    )(*scalars, *arrays)


def pair_step(index, rows, gate_mat, up_mat, acc):
    shape = ((rows.shape[0], gate_mat.shape[1]), jnp.float32)
    kernel = functools.partial(pair_kernel, not acc)
    return whole_call(kernel, "pair_step", [shape, shape], index, rows, gate_mat, up_mat, *acc)


def back_step(grads, down_mat, acc, last):
    rows, hidden_local = grads.shape[0], down_mat.shape[0]
    half = ((rows, hidden_local), jnp.bfloat16)
    if last:
        outs = [half, half, half, ((rows, LANES), jnp.float32)]
    else:
        outs = [((hidden_local, rows), jnp.float32)]
    kernel = functools.partial(back_kernel, not acc, bool(last))
    return whole_call(kernel, "back_step", outs, None, grads, down_mat, *acc, *last)


def piece_kernel(piece_ref, d_gate_ref, d_up_ref, slot_ref, gate_ref, up_ref, out_ref):
    piece = out_ref.shape[1] - LANES
    block = block_of(piece, 384)
    for i in range(piece // block):
        lines = pl.ds(pl.multiple_of(piece_ref[0] * piece + i * block, LANES), block)
        part = lax.dot_general(
            gate_ref[lines, :], d_gate_ref[...], LAST, preferred_element_type=jnp.float32
        ) + lax.dot_general(up_ref[lines, :], d_up_ref[...], LAST, preferred_element_type=jnp.float32)
        out_ref[:, i * block : (i + 1) * block] = part.T.astype(out_ref.dtype)
    out_ref[:, piece:] = slot_ref[...].astype(out_ref.dtype)


def row_piece(index, d_gate, d_up, slots, gate_mat, up_mat, piece, dtype):
    rows, hidden_local = d_gate.shape
    return pl.pallas_call(
        piece_kernel,
        in_specs=[pl.BlockSpec(memory_space=pltpu.SMEM)] + [pl.BlockSpec(memory_space=pltpu.VMEM)] * 5,
        out_specs=pl.BlockSpec(memory_space=pltpu.VMEM),
        out_shape=jax.ShapeDtypeStruct((rows, piece + LANES), dtype),
        compiler_params=pltpu.CompilerParams(vmem_limit_bytes=VMEM_LIMIT),
        cost_estimate=pl.CostEstimate(
            flops=4 * rows * hidden_local * piece,
            transcendentals=0,
            bytes_accessed=4 * hidden_local * (piece + rows),
        ),
        name="row_piece",
    )(index.reshape(1), d_gate, d_up, slots, gate_mat, up_mat)


def outer_kernel(left_ref, *refs):
    count = (len(refs) - 2) // 2
    rights, outs, held, sems = refs[:count], refs[count : 2 * count], refs[-2], refs[-1]
    slots, block, _ = held.shape
    copies = []
    for i in range(outs[0].shape[0] // block):
        left = left_ref[:, i * block : (i + 1) * block].T
        for right, out in zip(rights, outs):
            turn = len(copies)
            slot = turn % slots
            if turn >= slots:
                copies[turn - slots].wait()
            held[slot] = jnp.dot(left, right[...], preferred_element_type=jnp.float32).astype(
                held.dtype
            )
            copy = pltpu.make_async_copy(
                held.at[slot], out.at[pl.ds(i * block, block)], sems.at[slot]
            )
            copy.start()
            copies.append(copy)
    for copy in copies[-min(slots, len(copies)) :]:
        copy.wait()


def outer(left, *rights):
    height, width = left.shape[1], rights[0].shape[1]
    count = len(rights)
    block = block_of(height, max(LANES, 256 * 1024 // width // LANES * LANES))
    vmem = pl.BlockSpec(memory_space=pltpu.VMEM)
    slots = min(8, count * height // block)
    return pl.pallas_call(
        outer_kernel,
        in_specs=[vmem] * (1 + count),
        out_specs=[pl.BlockSpec(memory_space=pltpu.HBM)] * count,
        out_shape=[jax.ShapeDtypeStruct((height, width), jnp.bfloat16)] * count,
        scratch_shapes=[
            pltpu.VMEM((slots, block, width), jnp.bfloat16),
            pltpu.SemaphoreType.DMA((slots,)),
        ],
        compiler_params=pltpu.CompilerParams(vmem_limit_bytes=2 * VMEM_LIMIT),
        cost_estimate=pl.CostEstimate(
            flops=4 * count * left.shape[0] * height * width,
            transcendentals=0,
            bytes_accessed=2 * count * height * width,
        ),
        name="outer",
    )(left, *rights)


def on_device(tokens, out_grad, expert_ids, gate_probs, w_gate, w_up, w_down):
    expert = lax.axis_index("exp")
    hid = lax.axis_index("hid")
    tok_rows, model_width = tokens.shape
    capacity = 5 * tok_rows // 16
    seq_count = lax.axis_size("seq")
    hid_count = lax.axis_size("hid")
    piece = model_width // hid_count
    bf16, f32 = jnp.bfloat16, jnp.float32

    chosen = (expert_ids == expert).astype(jnp.int32)
    pick_own = pick_of(chosen, capacity)
    select_own = pick_own.astype(bf16)
    probs = jnp.sum(chosen * gate_probs, axis=1)
    weight_own = jnp.sum(jnp.where(pick_own, probs[:, None], 0.0), axis=0)

    def slots_of(x):
        return lax.dot_general(select_own, x, FIRST, preferred_element_type=f32)

    def row_slots(x):
        return slots_of(x).astype(bf16)

    def grad_slots(x):
        return (slots_of(x) * weight_own[:, None]).astype(bf16)

    def quarter(x):
        return lax.dynamic_slice_in_dim(x, hid * piece, piece, axis=1)

    def after(x, done):
        return lax.optimization_barrier((x, done))[0]

    def spread(x):
        return [swap(x, "seq", k) for k in range(1, seq_count)]

    def across(x):
        return [swap(x, "hid", j) for j in ((1, 2) if hid_count == 4 else range(1, hid_count))]

    remote = (seq_count - 1) * capacity
    split = -(-remote // 32) * 16

    def corner(one, two):
        if hid_count != 4:
            return []
        return [
            jnp.concatenate([swap(one[:split], "hid", 2), swap(two[split:], "hid", 1)], axis=0)
        ]

    def with_own(own, x, j):
        mine = lax.dynamic_slice_in_dim(own, (hid ^ j) * piece, piece, axis=1)
        return jnp.concatenate([mine, x], axis=0)

    row_message = row_slots(quarter(tokens))
    grad_message = after(grad_slots(quarter(out_grad)), row_message)
    own_rows, own_grads = after((row_slots(tokens), grad_slots(out_grad)), grad_message)
    gate_mat, up_mat, down_mat = w_gate[0], w_up[0], w_down[0]
    if seq_count == 4:
        row_two, row_one = swap(row_message, "seq", 2), swap(row_message, "seq", 1)
        grad_two, grad_one = swap(grad_message, "seq", 2), swap(grad_message, "seq", 1)
        row_two = after(row_two, (own_rows, own_grads))
        row_three = swap(row_two, "seq", 1)
        (gate_mat,) = fetch(after(gate_mat, row_two))
        grad_two = after(grad_two, gate_mat[:8, :LANES])
        grad_three = swap(grad_two, "seq", 1)
        row_blocks = after([row_one, row_two, row_three], grad_two)
        grad_blocks = [grad_one, grad_two, grad_three]
    else:
        row_blocks, grad_blocks = spread(row_message), spread(grad_message)
        (gate_mat,) = fetch(after(gate_mat, (own_rows, own_grads)))
        row_blocks = after(row_blocks, gate_mat[:8, :LANES])
    row_parts = [jnp.concatenate(row_blocks, axis=0)]
    row_across = across(row_parts[0])
    (up_mat,) = fetch(after(up_mat, row_parts[0]))
    grad_blocks = after(grad_blocks, up_mat[:8, :LANES])
    grad_parts = [jnp.concatenate(grad_blocks, axis=0)]
    grad_across = across(grad_parts[0])
    down = fetch_columns(hid, after(down_mat, grad_parts[0]), hid_count)
    pair = pair_step(
        hid, with_own(own_rows, after(row_parts[0], grad_parts[0]), 0), gate_mat, up_mat, ()
    )
    row_across = after(row_across, (grad_parts[0], pair, down[0][:8, :LANES]))
    row_corner = corner(row_across[0], row_across[1])
    for j, x in enumerate(row_across, 1):
        pair = pair_step(hid ^ j, with_own(own_rows, x, j), gate_mat, up_mat, pair)
    grad_across = after(grad_across, pair)
    grad_corner = corner(grad_across[0], grad_across[1])
    row_corner = after(row_corner, grad_across)
    for j, x in enumerate(row_corner, 3):
        pair = pair_step(hid ^ j, with_own(own_rows, x, j), gate_mat, up_mat, pair)
    back = back_step(with_own(own_grads, grad_parts[0], 0), down[0], (), ())
    rest = list(enumerate(grad_across, 1))
    if not grad_corner:
        final = rest.pop()
    for j, x in rest:
        back = back_step(with_own(own_grads, x, j), down[j], back, ())
    if grad_corner:
        final = (3, after(grad_corner[0], (back, pair)))
    row_parts += row_across + row_corner
    grad_parts += grad_across + grad_corner
    j, x = final
    hidden, d_gate, d_up, slots = back_step(
        with_own(own_grads, x, j), down[j], back, pair
    )

    def whole(own, parts):
        rest = jnp.zeros((remote, model_width), bf16)
        for j in range(hid_count):
            rest = lax.dynamic_update_slice_in_dim(rest, parts[j], (hid ^ j) * piece, axis=1)
        return jnp.concatenate([own, rest], axis=0)

    received = []
    source = (d_gate, d_up, slots)
    for j in range(hid_count - 1, -1, -1):
        part = row_piece(hid ^ j, *source, gate_mat, up_mat, piece, bf16 if j else f32)
        source = after(source, part)
        if j:
            received.append(swap(part, "hid", j))
    hidden, d_gate, d_up = after((hidden, d_gate, d_up), part)
    rows_e = whole(own_rows, after(row_parts, part))
    grads_e = whole(own_grads, after(grad_parts, part))
    grad_gate, grad_up = outer(rows_e, d_gate, d_up)
    if len(received) == 3:
        part = part + received[0].astype(f32)
        received = after(received[1:], part)
    received = after(received, (grad_gate, grad_up))
    block = (capacity, piece + LANES)
    own_sum, *messages = whole_call(
        sum_kernel, "sum_step", [(block, f32)] + [(block, bf16)] * (seq_count - 1), None, part, *received
    )
    (grad_down,) = outer(hidden, grads_e)
    arrived = [swap(message, "seq", k) for k, message in enumerate(messages, 1)]
    for part in after(arrived, grad_down):
        own_sum = own_sum + part.astype(f32)

    half = own_sum.astype(bf16)
    other_half = swap(half, "exp", 1)
    select_other = pick_of((expert_ids == 1 - expert).astype(jnp.int32), capacity).astype(bf16)
    d_tokens, d_gates = whole_call(
        place_kernel,
        "place_step",
        [((tok_rows, piece), f32), ((2, tok_rows), f32)],
        expert,
        expert_ids.T,
        gate_probs.T,
        select_own,
        select_other,
        half,
        other_half,
    )

    return (grad_gate[None], grad_up[None], grad_down[None], d_tokens, d_gates.T)


def solution(mesh):
    return jax.shard_map(
        on_device,
        mesh=mesh,
        in_specs=(
            P("seq", None),
            P("seq", None),
            P("seq", None),
            P("seq", None),
            P("exp", None, ("seq", "hid")),
            P("exp", None, ("seq", "hid")),
            P("exp", ("seq", "hid"), None),
        ),
        out_specs=(
            P("exp", None, ("seq", "hid")),
            P("exp", None, ("seq", "hid")),
            P("exp", ("seq", "hid"), None),
            P("seq", "hid"),
            P("seq", None),
        ),
        check_vma=False,
    )
```

```python
import functools

import functools

import jax
import jax.numpy as jnp
from jax import lax
from jax.experimental import pallas as pl
from jax.experimental.pallas import tpu as pltpu
from jax.sharding import PartitionSpec as P

LANES = 128
VMEM_LIMIT = 8 * 1024 * 1024
FETCH_PARTS = 8
LAST = (((1,), (1,)), ((), ()))
FIRST = (((0,), (0,)), ((), ()))


def swap(x, axis, bits):
    size = lax.axis_size(axis)
    return lax.ppermute(x, axis, [(i, i ^ bits) for i in range(size)])


def block_of(extent, most):
    size = most
    while extent % size:
        size -= LANES
    return size


def pick_of(chosen, capacity):
    named = jnp.sum(chosen, axis=1)
    place = jnp.arange(chosen.shape[0], dtype=jnp.int32)
    slot = jnp.sum(jnp.where(place[None, :] < place[:, None], named[None, :], 0), axis=1)
    columns = jnp.arange(capacity, dtype=jnp.int32)
    return (named[:, None] > 0) & (slot[:, None] == columns[None, :])


def place_kernel(
    expert_ref, ids_ref, probs_ref, own_ref, other_ref, half_ref, other_half_ref,
    tokens_ref, gates_ref,
):
    piece = tokens_ref.shape[1]
    own, other = own_ref[...], other_ref[...]
    half, other_half = half_ref[...], other_half_ref[...]
    tokens_ref[...] = jnp.dot(own, half[:, :piece], preferred_element_type=jnp.float32) + jnp.dot(
        other, other_half[:, :piece], preferred_element_type=jnp.float32
    )
    ids = ids_ref[...]

    def gates(select, sums, expert):
        token = lax.dot_general(
            sums[:, piece:], select, (((0,), (1,)), ((), ())), preferred_element_type=jnp.float32
        )
        return jnp.where(ids == expert, token[:1], 0.0)

    mine = expert_ref[0]
    gates_ref[...] = (gates(own, half, mine) + gates(other, other_half, 1 - mine)) / probs_ref[...]


def sum_kernel(own_ref, *refs):
    capacity = refs[-1].shape[0]
    first = len(refs) - own_ref.shape[0] // capacity
    parts, outs = refs[:first], refs[first:]
    for k, out in enumerate(outs):
        lines = slice(k * capacity, (k + 1) * capacity)
        total = own_ref[lines, :]
        for part in parts:
            total = total + part[lines, :].astype(jnp.float32)
        out[...] = total.astype(out.dtype)


def fetch_kernel(*refs):
    count = (len(refs) - 1) // 2
    sources, targets, sems = refs[:count], refs[count : 2 * count], refs[-1]
    copies = []
    for m in range(count):
        lines = sources[m].shape[0] // FETCH_PARTS
        for i in range(FETCH_PARTS):
            part = pl.ds(i * lines, lines)
            copies.append(
                pltpu.make_async_copy(sources[m].at[part], targets[m].at[part], sems.at[m, i])
            )
    for copy in copies:
        copy.start()
    for copy in copies:
        copy.wait()


def fetch(*arrays):
    return pl.pallas_call(
        fetch_kernel,
        in_specs=[pl.BlockSpec(memory_space=pltpu.HBM)] * len(arrays),
        out_specs=[pl.BlockSpec(memory_space=pltpu.VMEM)] * len(arrays),
        out_shape=[pltpu.VMEM(x.shape, x.dtype) for x in arrays],
        scratch_shapes=[pltpu.SemaphoreType.DMA((len(arrays), FETCH_PARTS))],
        compiler_params=pltpu.CompilerParams(vmem_limit_bytes=VMEM_LIMIT),
        name="fetch",
    )(*(pltpu.with_memory_space_constraint(x, pltpu.HBM) for x in arrays))


def columns_kernel(index_ref, source_ref, *refs):
    targets, sems = refs[:-1], refs[-1]
    height, width = targets[0].shape
    lines = height // FETCH_PARTS
    copies = []
    for j, target in enumerate(targets):
        start = pl.multiple_of((index_ref[0] ^ j) * width, LANES)
        for i in range(FETCH_PARTS):
            part = pl.ds(i * lines, lines)
            copies.append(
                pltpu.make_async_copy(
                    source_ref.at[part, pl.ds(start, width)], target.at[part], sems.at[j, i]
                )
            )
    for copy in copies:
        copy.start()
    for copy in copies:
        copy.wait()


def fetch_columns(index, array, count):
    height, width = array.shape[0], array.shape[1] // count
    return pl.pallas_call(
        columns_kernel,
        in_specs=[
            pl.BlockSpec(memory_space=pltpu.SMEM),
            pl.BlockSpec(memory_space=pltpu.HBM),
        ],
        out_specs=[pl.BlockSpec(memory_space=pltpu.VMEM)] * count,
        out_shape=[pltpu.VMEM((height, width), array.dtype)] * count,
        scratch_shapes=[pltpu.SemaphoreType.DMA((count, FETCH_PARTS))],
        compiler_params=pltpu.CompilerParams(vmem_limit_bytes=VMEM_LIMIT),
        name="fetch_columns",
    )(index.reshape(1), pltpu.with_memory_space_constraint(array, pltpu.HBM))


def pair_kernel(first, index_ref, rows_ref, gate_ref, up_ref, *refs):
    piece = rows_ref.shape[1]
    block = block_of(piece, 512)
    gate_out, up_out = refs[-2:]
    gate, up = (None, None) if first else (refs[0][...], refs[1][...])
    for i in range(piece // block):
        lines = pl.ds(pl.multiple_of(index_ref[0] * piece + i * block, LANES), block)
        rows = rows_ref[:, i * block : (i + 1) * block]
        more_gate = jnp.dot(rows, gate_ref[lines, :], preferred_element_type=jnp.float32)
        more_up = jnp.dot(rows, up_ref[lines, :], preferred_element_type=jnp.float32)
        gate = more_gate if gate is None else gate + more_gate
        up = more_up if up is None else up + more_up
    gate_out[...] = gate
    up_out[...] = up


def back_kernel(first, last, grads_ref, down_ref, *refs):
    piece = grads_ref.shape[1]
    block = block_of(piece, 512)
    back = None if first else refs[0][...]
    for i in range(piece // block):
        lines = slice(i * block, (i + 1) * block)
        grads = grads_ref[:, lines]
        more = lax.dot_general(
            down_ref[:, lines], grads, LAST, preferred_element_type=jnp.float32
        )
        back = more if back is None else back + more
    if not last:
        refs[-1][...] = back
        return
    gate_ref, up_ref, hidden_ref, d_gate_ref, d_up_ref, slot_ref = refs[-6:]
    back = back.T
    gate = gate_ref[...]
    up = up_ref[...]
    sig = jax.nn.sigmoid(gate)
    activated = gate * sig
    hidden = (activated * up).astype(jnp.bfloat16)
    hidden_ref[...] = hidden
    slots = jnp.sum(hidden.astype(jnp.float32) * back, axis=1, keepdims=True)
    slot_ref[...] = jnp.broadcast_to(slots, slot_ref.shape)
    d_gate_ref[...] = (back * up * (sig * (1.0 + gate * (1.0 - sig)))).astype(jnp.bfloat16)
    d_up_ref[...] = (back * activated).astype(jnp.bfloat16)


def whole_call(kernel, name, outs, index, *arrays):
    scalars = [] if index is None else [index.reshape(1)]
    return pl.pallas_call(
        kernel,
        in_specs=[pl.BlockSpec(memory_space=pltpu.SMEM)] * len(scalars)
        + [pl.BlockSpec(memory_space=pltpu.VMEM)] * len(arrays),
        out_specs=[pl.BlockSpec(memory_space=pltpu.VMEM)] * len(outs),
        out_shape=[jax.ShapeDtypeStruct(*x) for x in outs],
        compiler_params=pltpu.CompilerParams(vmem_limit_bytes=VMEM_LIMIT),
        name=name,
    )(*scalars, *arrays)


def pair_step(index, rows, gate_mat, up_mat, acc):
    shape = ((rows.shape[0], gate_mat.shape[1]), jnp.float32)
    kernel = functools.partial(pair_kernel, not acc)
    return whole_call(kernel, "pair_step", [shape, shape], index, rows, gate_mat, up_mat, *acc)


def back_step(grads, down_mat, acc, last):
    rows, hidden_local = grads.shape[0], down_mat.shape[0]
    half = ((rows, hidden_local), jnp.bfloat16)
    if last:
        outs = [half, half, half, ((rows, LANES), jnp.float32)]
    else:
        outs = [((hidden_local, rows), jnp.float32)]
    kernel = functools.partial(back_kernel, not acc, bool(last))
    return whole_call(kernel, "back_step", outs, None, grads, down_mat, *acc, *last)


def piece_kernel(piece_ref, d_gate_ref, d_up_ref, slot_ref, gate_ref, up_ref, out_ref):
    piece = out_ref.shape[1] - LANES
    block = block_of(piece, 384)
    for i in range(piece // block):
        lines = pl.ds(pl.multiple_of(piece_ref[0] * piece + i * block, LANES), block)
        part = lax.dot_general(
            gate_ref[lines, :], d_gate_ref[...], LAST, preferred_element_type=jnp.float32
        ) + lax.dot_general(up_ref[lines, :], d_up_ref[...], LAST, preferred_element_type=jnp.float32)
        out_ref[:, i * block : (i + 1) * block] = part.T.astype(out_ref.dtype)
    out_ref[:, piece:] = slot_ref[...].astype(out_ref.dtype)


def row_piece(index, d_gate, d_up, slots, gate_mat, up_mat, piece, dtype):
    rows, hidden_local = d_gate.shape
    return pl.pallas_call(
        piece_kernel,
        in_specs=[pl.BlockSpec(memory_space=pltpu.SMEM)] + [pl.BlockSpec(memory_space=pltpu.VMEM)] * 5,
        out_specs=pl.BlockSpec(memory_space=pltpu.VMEM),
        out_shape=jax.ShapeDtypeStruct((rows, piece + LANES), dtype),
        compiler_params=pltpu.CompilerParams(vmem_limit_bytes=VMEM_LIMIT),
        cost_estimate=pl.CostEstimate(
            flops=4 * rows * hidden_local * piece,
            transcendentals=0,
            bytes_accessed=4 * hidden_local * (piece + rows),
        ),
        name="row_piece",
    )(index.reshape(1), d_gate, d_up, slots, gate_mat, up_mat)


def outer_kernel(left_ref, *refs):
    count = (len(refs) - 2) // 2
    rights, outs, held, sems = refs[:count], refs[count : 2 * count], refs[-2], refs[-1]
    slots, block, _ = held.shape
    copies = []
    for i in range(outs[0].shape[0] // block):
        left = left_ref[:, i * block : (i + 1) * block].T
        for right, out in zip(rights, outs):
            turn = len(copies)
            slot = turn % slots
            if turn >= slots:
                copies[turn - slots].wait()
            held[slot] = jnp.dot(left, right[...], preferred_element_type=jnp.float32).astype(
                held.dtype
            )
            copy = pltpu.make_async_copy(
                held.at[slot], out.at[pl.ds(i * block, block)], sems.at[slot]
            )
            copy.start()
            copies.append(copy)
    for copy in copies[-min(slots, len(copies)) :]:
        copy.wait()


def outer(left, *rights):
    height, width = left.shape[1], rights[0].shape[1]
    count = len(rights)
    block = block_of(height, max(LANES, 256 * 1024 // width // LANES * LANES))
    vmem = pl.BlockSpec(memory_space=pltpu.VMEM)
    slots = min(8, count * height // block)
    return pl.pallas_call(
        outer_kernel,
        in_specs=[vmem] * (1 + count),
        out_specs=[pl.BlockSpec(memory_space=pltpu.HBM)] * count,
        out_shape=[jax.ShapeDtypeStruct((height, width), jnp.bfloat16)] * count,
        scratch_shapes=[
            pltpu.VMEM((slots, block, width), jnp.bfloat16),
            pltpu.SemaphoreType.DMA((slots,)),
        ],
        compiler_params=pltpu.CompilerParams(vmem_limit_bytes=2 * VMEM_LIMIT),
        cost_estimate=pl.CostEstimate(
            flops=4 * count * left.shape[0] * height * width,
            transcendentals=0,
            bytes_accessed=2 * count * height * width,
        ),
        name="outer",
    )(left, *rights)


def on_device(tokens, out_grad, expert_ids, gate_probs, w_gate, w_up, w_down):
    expert = lax.axis_index("exp")
    hid = lax.axis_index("hid")
    tok_rows, model_width = tokens.shape
    capacity = 5 * tok_rows // 16
    seq_count = lax.axis_size("seq")
    hid_count = lax.axis_size("hid")
    piece = model_width // hid_count
    bf16, f32 = jnp.bfloat16, jnp.float32

    chosen = (expert_ids == expert).astype(jnp.int32)
    pick_own = pick_of(chosen, capacity)
    select_own = pick_own.astype(bf16)
    probs = jnp.sum(chosen * gate_probs, axis=1)
    weight_own = jnp.sum(jnp.where(pick_own, probs[:, None], 0.0), axis=0)

    def slots_of(x):
        return lax.dot_general(select_own, x, FIRST, preferred_element_type=f32)

    def row_slots(x):
        return slots_of(x).astype(bf16)

    def grad_slots(x):
        return (slots_of(x) * weight_own[:, None]).astype(bf16)

    def quarter(x):
        return lax.dynamic_slice_in_dim(x, hid * piece, piece, axis=1)

    def after(x, done):
        return lax.optimization_barrier((x, done))[0]

    def spread(x):
        return [swap(x, "seq", k) for k in range(1, seq_count)]

    def across(x):
        return [swap(x, "hid", j) for j in ((1, 2) if hid_count == 4 else range(1, hid_count))]

    remote = (seq_count - 1) * capacity
    split = -(-remote // 32) * 16

    def corner(one, two):
        if hid_count != 4:
            return []
        return [
            jnp.concatenate([swap(one[:split], "hid", 2), swap(two[split:], "hid", 1)], axis=0)
        ]

    def with_own(own, x, j):
        mine = lax.dynamic_slice_in_dim(own, (hid ^ j) * piece, piece, axis=1)
        return jnp.concatenate([mine, x], axis=0)

    row_message = row_slots(quarter(tokens))
    grad_message = after(grad_slots(quarter(out_grad)), row_message)
    own_rows, own_grads = after((row_slots(tokens), grad_slots(out_grad)), grad_message)
    gate_mat, up_mat, down_mat = w_gate[0], w_up[0], w_down[0]
    if seq_count == 4:
        row_two, row_one = swap(row_message, "seq", 2), swap(row_message, "seq", 1)
        grad_two, grad_one = swap(grad_message, "seq", 2), swap(grad_message, "seq", 1)
        row_two = after(row_two, (own_rows, own_grads))
        row_three = swap(row_two, "seq", 1)
        (gate_mat,) = fetch(after(gate_mat, row_two))
        grad_two = after(grad_two, gate_mat[:8, :LANES])
        grad_three = swap(grad_two, "seq", 1)
        row_blocks = after([row_one, row_two, row_three], grad_two)
        grad_blocks = [grad_one, grad_two, grad_three]
    else:
        row_blocks, grad_blocks = spread(row_message), spread(grad_message)
        (gate_mat,) = fetch(after(gate_mat, (own_rows, own_grads)))
        row_blocks = after(row_blocks, gate_mat[:8, :LANES])
    row_parts = [jnp.concatenate(row_blocks, axis=0)]
    row_across = across(row_parts[0])
    (up_mat,) = fetch(after(up_mat, row_parts[0]))
    grad_blocks = after(grad_blocks, up_mat[:8, :LANES])
    grad_parts = [jnp.concatenate(grad_blocks, axis=0)]
    grad_across = across(grad_parts[0])
    down = fetch_columns(hid, after(down_mat, grad_parts[0]), hid_count)
    pair = pair_step(
        hid, with_own(own_rows, after(row_parts[0], grad_parts[0]), 0), gate_mat, up_mat, ()
    )
    row_across = after(row_across, (grad_parts[0], pair, down[0][:8, :LANES]))
    row_corner = corner(row_across[0], row_across[1])
    for j, x in enumerate(row_across, 1):
        pair = pair_step(hid ^ j, with_own(own_rows, x, j), gate_mat, up_mat, pair)
    grad_across = after(grad_across, pair)
    grad_corner = corner(grad_across[0], grad_across[1])
    row_corner = after(row_corner, grad_across)
    for j, x in enumerate(row_corner, 3):
        pair = pair_step(hid ^ j, with_own(own_rows, x, j), gate_mat, up_mat, pair)
    back = back_step(with_own(own_grads, grad_parts[0], 0), down[0], (), ())
    rest = list(enumerate(grad_across, 1))
    if not grad_corner:
        final = rest.pop()
    for j, x in rest:
        back = back_step(with_own(own_grads, x, j), down[j], back, ())
    if grad_corner:
        final = (3, after(grad_corner[0], (back, pair)))
    row_parts += row_across + row_corner
    grad_parts += grad_across + grad_corner
    j, x = final
    hidden, d_gate, d_up, slots = back_step(
        with_own(own_grads, x, j), down[j], back, pair
    )

    def whole(own, parts):
        rest = jnp.zeros((remote, model_width), bf16)
        for j in range(hid_count):
            rest = lax.dynamic_update_slice_in_dim(rest, parts[j], (hid ^ j) * piece, axis=1)
        return jnp.concatenate([own, rest], axis=0)

    received = []
    source = (d_gate, d_up, slots)
    for j in range(hid_count - 1, -1, -1):
        part = row_piece(hid ^ j, *source, gate_mat, up_mat, piece, bf16 if j else f32)
        source = after(source, part)
        if j:
            received.append(swap(part, "hid", j))
    hidden, d_gate, d_up = after((hidden, d_gate, d_up), part)
    rows_e = whole(own_rows, after(row_parts, part))
    grads_e = whole(own_grads, after(grad_parts, part))
    (grad_gate,) = outer(rows_e, d_gate)
    (grad_down,) = outer(hidden, grads_e)
    if len(received) == 3:
        part = part + received[0].astype(f32)
        received = after(received[1:], part)
    received = after(received, (grad_gate, grad_down))
    block = (capacity, piece + LANES)
    own_sum, *messages = whole_call(
        sum_kernel, "sum_step", [(block, f32)] + [(block, bf16)] * (seq_count - 1), None, part, *received
    )
    (grad_up,) = outer(rows_e, d_up)
    arrived = [swap(message, "seq", k) for k, message in enumerate(messages, 1)]
    for part in after(arrived, grad_up):
        own_sum = own_sum + part.astype(f32)

    half = own_sum.astype(bf16)
    other_half = swap(half, "exp", 1)
    select_other = pick_of((expert_ids == 1 - expert).astype(jnp.int32), capacity).astype(bf16)
    d_tokens, d_gates = whole_call(
        place_kernel,
        "place_step",
        [((tok_rows, piece), f32), ((2, tok_rows), f32)],
        expert,
        expert_ids.T,
        gate_probs.T,
        select_own,
        select_other,
        half,
        other_half,
    )

    return (grad_gate[None], grad_up[None], grad_down[None], d_tokens, d_gates.T)


def solution(mesh):
    return jax.shard_map(
        on_device,
        mesh=mesh,
        in_specs=(
            P("seq", None),
            P("seq", None),
            P("seq", None),
            P("seq", None),
            P("exp", None, ("seq", "hid")),
            P("exp", None, ("seq", "hid")),
            P("exp", ("seq", "hid"), None),
        ),
        out_specs=(
            P("exp", None, ("seq", "hid")),
            P("exp", None, ("seq", "hid")),
            P("exp", ("seq", "hid"), None),
            P("seq", "hid"),
            P("seq", None),
        ),
        check_vma=False,
    )
```

```python
import functools

import functools

import jax
import jax.numpy as jnp
from jax import lax
from jax.experimental import pallas as pl
from jax.experimental.pallas import tpu as pltpu
from jax.sharding import PartitionSpec as P

LANES = 128
VMEM_LIMIT = 8 * 1024 * 1024
FETCH_PARTS = 8
LAST = (((1,), (1,)), ((), ()))
FIRST = (((0,), (0,)), ((), ()))


def swap(x, axis, bits):
    size = lax.axis_size(axis)
    return lax.ppermute(x, axis, [(i, i ^ bits) for i in range(size)])


def block_of(extent, most):
    size = most
    while extent % size:
        size -= LANES
    return size


def pick_of(chosen, capacity):
    named = jnp.sum(chosen, axis=1)
    place = jnp.arange(chosen.shape[0], dtype=jnp.int32)
    slot = jnp.sum(jnp.where(place[None, :] < place[:, None], named[None, :], 0), axis=1)
    columns = jnp.arange(capacity, dtype=jnp.int32)
    return (named[:, None] > 0) & (slot[:, None] == columns[None, :])


def place_kernel(
    expert_ref, ids_ref, probs_ref, own_ref, other_ref, half_ref, other_half_ref,
    tokens_ref, gates_ref,
):
    piece = tokens_ref.shape[1]
    own, other = own_ref[...], other_ref[...]
    half, other_half = half_ref[...], other_half_ref[...]
    tokens_ref[...] = jnp.dot(own, half[:, :piece], preferred_element_type=jnp.float32) + jnp.dot(
        other, other_half[:, :piece], preferred_element_type=jnp.float32
    )
    ids = ids_ref[...]

    def gates(select, sums, expert):
        token = lax.dot_general(
            sums[:, piece:], select, (((0,), (1,)), ((), ())), preferred_element_type=jnp.float32
        )
        return jnp.where(ids == expert, token[:1], 0.0)

    mine = expert_ref[0]
    gates_ref[...] = (gates(own, half, mine) + gates(other, other_half, 1 - mine)) / probs_ref[...]


def sum_kernel(own_ref, *refs):
    capacity = refs[-1].shape[0]
    first = len(refs) - own_ref.shape[0] // capacity
    parts, outs = refs[:first], refs[first:]
    for k, out in enumerate(outs):
        lines = slice(k * capacity, (k + 1) * capacity)
        total = own_ref[lines, :]
        for part in parts:
            total = total + part[lines, :].astype(jnp.float32)
        out[...] = total.astype(out.dtype)


def fetch_kernel(*refs):
    count = (len(refs) - 1) // 2
    sources, targets, sems = refs[:count], refs[count : 2 * count], refs[-1]
    copies = []
    for m in range(count):
        lines = sources[m].shape[0] // FETCH_PARTS
        for i in range(FETCH_PARTS):
            part = pl.ds(i * lines, lines)
            copies.append(
                pltpu.make_async_copy(sources[m].at[part], targets[m].at[part], sems.at[m, i])
            )
    for copy in copies:
        copy.start()
    for copy in copies:
        copy.wait()


def fetch(*arrays):
    return pl.pallas_call(
        fetch_kernel,
        in_specs=[pl.BlockSpec(memory_space=pltpu.HBM)] * len(arrays),
        out_specs=[pl.BlockSpec(memory_space=pltpu.VMEM)] * len(arrays),
        out_shape=[pltpu.VMEM(x.shape, x.dtype) for x in arrays],
        scratch_shapes=[pltpu.SemaphoreType.DMA((len(arrays), FETCH_PARTS))],
        compiler_params=pltpu.CompilerParams(vmem_limit_bytes=VMEM_LIMIT),
        name="fetch",
    )(*(pltpu.with_memory_space_constraint(x, pltpu.HBM) for x in arrays))


def columns_kernel(index_ref, source_ref, *refs):
    targets, sems = refs[:-1], refs[-1]
    height, width = targets[0].shape
    lines = height // FETCH_PARTS
    copies = []
    for j, target in enumerate(targets):
        start = pl.multiple_of((index_ref[0] ^ j) * width, LANES)
        for i in range(FETCH_PARTS):
            part = pl.ds(i * lines, lines)
            copies.append(
                pltpu.make_async_copy(
                    source_ref.at[part, pl.ds(start, width)], target.at[part], sems.at[j, i]
                )
            )
    for copy in copies:
        copy.start()
    for copy in copies:
        copy.wait()


def fetch_columns(index, array, count):
    height, width = array.shape[0], array.shape[1] // count
    return pl.pallas_call(
        columns_kernel,
        in_specs=[
            pl.BlockSpec(memory_space=pltpu.SMEM),
            pl.BlockSpec(memory_space=pltpu.HBM),
        ],
        out_specs=[pl.BlockSpec(memory_space=pltpu.VMEM)] * count,
        out_shape=[pltpu.VMEM((height, width), array.dtype)] * count,
        scratch_shapes=[pltpu.SemaphoreType.DMA((count, FETCH_PARTS))],
        compiler_params=pltpu.CompilerParams(vmem_limit_bytes=VMEM_LIMIT),
        name="fetch_columns",
    )(index.reshape(1), pltpu.with_memory_space_constraint(array, pltpu.HBM))


def pair_kernel(first, index_ref, rows_ref, gate_ref, up_ref, *refs):
    piece = rows_ref.shape[1]
    block = block_of(piece, 512)
    gate_out, up_out = refs[-2:]
    gate, up = (None, None) if first else (refs[0][...], refs[1][...])
    for i in range(piece // block):
        lines = pl.ds(pl.multiple_of(index_ref[0] * piece + i * block, LANES), block)
        rows = rows_ref[:, i * block : (i + 1) * block]
        more_gate = jnp.dot(rows, gate_ref[lines, :], preferred_element_type=jnp.float32)
        more_up = jnp.dot(rows, up_ref[lines, :], preferred_element_type=jnp.float32)
        gate = more_gate if gate is None else gate + more_gate
        up = more_up if up is None else up + more_up
    gate_out[...] = gate
    up_out[...] = up


def back_kernel(first, last, grads_ref, down_ref, *refs):
    piece = grads_ref.shape[1]
    block = block_of(piece, 512)
    back = None if first else refs[0][...]
    for i in range(piece // block):
        lines = slice(i * block, (i + 1) * block)
        grads = grads_ref[:, lines]
        more = lax.dot_general(
            down_ref[:, lines], grads, LAST, preferred_element_type=jnp.float32
        )
        back = more if back is None else back + more
    if not last:
        refs[-1][...] = back
        return
    gate_ref, up_ref, hidden_ref, d_gate_ref, d_up_ref, slot_ref = refs[-6:]
    back = back.T
    gate = gate_ref[...]
    up = up_ref[...]
    sig = jax.nn.sigmoid(gate)
    activated = gate * sig
    hidden = (activated * up).astype(jnp.bfloat16)
    hidden_ref[...] = hidden
    slots = jnp.sum(hidden.astype(jnp.float32) * back, axis=1, keepdims=True)
    slot_ref[...] = jnp.broadcast_to(slots, slot_ref.shape)
    d_gate_ref[...] = (back * up * (sig * (1.0 + gate * (1.0 - sig)))).astype(jnp.bfloat16)
    d_up_ref[...] = (back * activated).astype(jnp.bfloat16)


def whole_call(kernel, name, outs, index, *arrays):
    scalars = [] if index is None else [index.reshape(1)]
    return pl.pallas_call(
        kernel,
        in_specs=[pl.BlockSpec(memory_space=pltpu.SMEM)] * len(scalars)
        + [pl.BlockSpec(memory_space=pltpu.VMEM)] * len(arrays),
        out_specs=[pl.BlockSpec(memory_space=pltpu.VMEM)] * len(outs),
        out_shape=[jax.ShapeDtypeStruct(*x) for x in outs],
        compiler_params=pltpu.CompilerParams(vmem_limit_bytes=VMEM_LIMIT),
        name=name,
    )(*scalars, *arrays)


def pair_step(index, rows, gate_mat, up_mat, acc):
    shape = ((rows.shape[0], gate_mat.shape[1]), jnp.float32)
    kernel = functools.partial(pair_kernel, not acc)
    return whole_call(kernel, "pair_step", [shape, shape], index, rows, gate_mat, up_mat, *acc)


def back_step(grads, down_mat, acc, last):
    rows, hidden_local = grads.shape[0], down_mat.shape[0]
    half = ((rows, hidden_local), jnp.bfloat16)
    if last:
        outs = [half, half, half, ((rows, LANES), jnp.float32)]
    else:
        outs = [((hidden_local, rows), jnp.float32)]
    kernel = functools.partial(back_kernel, not acc, bool(last))
    return whole_call(kernel, "back_step", outs, None, grads, down_mat, *acc, *last)


def piece_kernel(piece_ref, d_gate_ref, d_up_ref, slot_ref, gate_ref, up_ref, out_ref):
    piece = out_ref.shape[1] - LANES
    block = block_of(piece, 384)
    for i in range(piece // block):
        lines = pl.ds(pl.multiple_of(piece_ref[0] * piece + i * block, LANES), block)
        part = lax.dot_general(
            gate_ref[lines, :], d_gate_ref[...], LAST, preferred_element_type=jnp.float32
        ) + lax.dot_general(up_ref[lines, :], d_up_ref[...], LAST, preferred_element_type=jnp.float32)
        out_ref[:, i * block : (i + 1) * block] = part.T.astype(out_ref.dtype)
    out_ref[:, piece:] = slot_ref[...].astype(out_ref.dtype)


def row_piece(index, d_gate, d_up, slots, gate_mat, up_mat, piece, dtype):
    rows, hidden_local = d_gate.shape
    return pl.pallas_call(
        piece_kernel,
        in_specs=[pl.BlockSpec(memory_space=pltpu.SMEM)] + [pl.BlockSpec(memory_space=pltpu.VMEM)] * 5,
        out_specs=pl.BlockSpec(memory_space=pltpu.VMEM),
        out_shape=jax.ShapeDtypeStruct((rows, piece + LANES), dtype),
        compiler_params=pltpu.CompilerParams(vmem_limit_bytes=VMEM_LIMIT),
        cost_estimate=pl.CostEstimate(
            flops=4 * rows * hidden_local * piece,
            transcendentals=0,
            bytes_accessed=4 * hidden_local * (piece + rows),
        ),
        name="row_piece",
    )(index.reshape(1), d_gate, d_up, slots, gate_mat, up_mat)


def outer_kernel(left_ref, *refs):
    count = (len(refs) - 2) // 2
    rights, outs, held, sems = refs[:count], refs[count : 2 * count], refs[-2], refs[-1]
    slots, block, _ = held.shape
    copies = []
    for i in range(outs[0].shape[0] // block):
        left = left_ref[:, i * block : (i + 1) * block].T
        for right, out in zip(rights, outs):
            turn = len(copies)
            slot = turn % slots
            if turn >= slots:
                copies[turn - slots].wait()
            held[slot] = jnp.dot(left, right[...], preferred_element_type=jnp.float32).astype(
                held.dtype
            )
            copy = pltpu.make_async_copy(
                held.at[slot], out.at[pl.ds(i * block, block)], sems.at[slot]
            )
            copy.start()
            copies.append(copy)
    for copy in copies[-min(slots, len(copies)) :]:
        copy.wait()


def outer(left, *rights):
    height, width = left.shape[1], rights[0].shape[1]
    count = len(rights)
    block = block_of(height, max(LANES, 512 * 1024 // width // LANES * LANES))
    vmem = pl.BlockSpec(memory_space=pltpu.VMEM)
    slots = min(6, count * height // block)
    return pl.pallas_call(
        outer_kernel,
        in_specs=[vmem] * (1 + count),
        out_specs=[pl.BlockSpec(memory_space=pltpu.HBM)] * count,
        out_shape=[jax.ShapeDtypeStruct((height, width), jnp.bfloat16)] * count,
        scratch_shapes=[
            pltpu.VMEM((slots, block, width), jnp.bfloat16),
            pltpu.SemaphoreType.DMA((slots,)),
        ],
        compiler_params=pltpu.CompilerParams(vmem_limit_bytes=2 * VMEM_LIMIT),
        cost_estimate=pl.CostEstimate(
            flops=4 * count * left.shape[0] * height * width,
            transcendentals=0,
            bytes_accessed=2 * count * height * width,
        ),
        name="outer",
    )(left, *rights)


def on_device(tokens, out_grad, expert_ids, gate_probs, w_gate, w_up, w_down):
    expert = lax.axis_index("exp")
    hid = lax.axis_index("hid")
    tok_rows, model_width = tokens.shape
    capacity = 5 * tok_rows // 16
    seq_count = lax.axis_size("seq")
    hid_count = lax.axis_size("hid")
    piece = model_width // hid_count
    bf16, f32 = jnp.bfloat16, jnp.float32

    chosen = (expert_ids == expert).astype(jnp.int32)
    pick_own = pick_of(chosen, capacity)
    select_own = pick_own.astype(bf16)
    probs = jnp.sum(chosen * gate_probs, axis=1)
    weight_own = jnp.sum(jnp.where(pick_own, probs[:, None], 0.0), axis=0)

    def slots_of(x):
        return lax.dot_general(select_own, x, FIRST, preferred_element_type=f32)

    def row_slots(x):
        return slots_of(x).astype(bf16)

    def grad_slots(x):
        return (slots_of(x) * weight_own[:, None]).astype(bf16)

    def quarter(x):
        return lax.dynamic_slice_in_dim(x, hid * piece, piece, axis=1)

    def after(x, done):
        return lax.optimization_barrier((x, done))[0]

    def spread(x):
        return [swap(x, "seq", k) for k in range(1, seq_count)]

    def across(x):
        return [swap(x, "hid", j) for j in ((1, 2) if hid_count == 4 else range(1, hid_count))]

    remote = (seq_count - 1) * capacity
    split = -(-remote // 32) * 16

    def corner(one, two):
        if hid_count != 4:
            return []
        return [
            jnp.concatenate([swap(one[:split], "hid", 2), swap(two[split:], "hid", 1)], axis=0)
        ]

    def with_own(own, x, j):
        mine = lax.dynamic_slice_in_dim(own, (hid ^ j) * piece, piece, axis=1)
        return jnp.concatenate([mine, x], axis=0)

    row_message = row_slots(quarter(tokens))
    grad_message = after(grad_slots(quarter(out_grad)), row_message)
    own_rows, own_grads = after((row_slots(tokens), grad_slots(out_grad)), grad_message)
    gate_mat, up_mat, down_mat = w_gate[0], w_up[0], w_down[0]
    if seq_count == 4:
        row_two, row_one = swap(row_message, "seq", 2), swap(row_message, "seq", 1)
        grad_two, grad_one = swap(grad_message, "seq", 2), swap(grad_message, "seq", 1)
        row_two = after(row_two, (own_rows, own_grads))
        row_three = swap(row_two, "seq", 1)
        (gate_mat,) = fetch(after(gate_mat, row_two))
        grad_two = after(grad_two, gate_mat[:8, :LANES])
        grad_three = swap(grad_two, "seq", 1)
        row_blocks = after([row_one, row_two, row_three], grad_two)
        grad_blocks = [grad_one, grad_two, grad_three]
    else:
        row_blocks, grad_blocks = spread(row_message), spread(grad_message)
        (gate_mat,) = fetch(after(gate_mat, (own_rows, own_grads)))
        row_blocks = after(row_blocks, gate_mat[:8, :LANES])
    row_parts = [jnp.concatenate(row_blocks, axis=0)]
    row_across = across(row_parts[0])
    (up_mat,) = fetch(after(up_mat, row_parts[0]))
    grad_blocks = after(grad_blocks, up_mat[:8, :LANES])
    grad_parts = [jnp.concatenate(grad_blocks, axis=0)]
    grad_across = across(grad_parts[0])
    down = fetch_columns(hid, after(down_mat, grad_parts[0]), hid_count)
    pair = pair_step(
        hid, with_own(own_rows, after(row_parts[0], grad_parts[0]), 0), gate_mat, up_mat, ()
    )
    row_across = after(row_across, (grad_parts[0], pair, down[0][:8, :LANES]))
    row_corner = corner(row_across[0], row_across[1])
    for j, x in enumerate(row_across, 1):
        pair = pair_step(hid ^ j, with_own(own_rows, x, j), gate_mat, up_mat, pair)
    grad_across = after(grad_across, pair)
    grad_corner = corner(grad_across[0], grad_across[1])
    row_corner = after(row_corner, grad_across)
    for j, x in enumerate(row_corner, 3):
        pair = pair_step(hid ^ j, with_own(own_rows, x, j), gate_mat, up_mat, pair)
    back = back_step(with_own(own_grads, grad_parts[0], 0), down[0], (), ())
    rest = list(enumerate(grad_across, 1))
    if not grad_corner:
        final = rest.pop()
    for j, x in rest:
        back = back_step(with_own(own_grads, x, j), down[j], back, ())
    if grad_corner:
        final = (3, after(grad_corner[0], (back, pair)))
    row_parts += row_across + row_corner
    grad_parts += grad_across + grad_corner
    j, x = final
    hidden, d_gate, d_up, slots = back_step(
        with_own(own_grads, x, j), down[j], back, pair
    )

    def whole(own, parts):
        rest = jnp.zeros((remote, model_width), bf16)
        for j in range(hid_count):
            rest = lax.dynamic_update_slice_in_dim(rest, parts[j], (hid ^ j) * piece, axis=1)
        return jnp.concatenate([own, rest], axis=0)

    received = []
    source = (d_gate, d_up, slots)
    for j in range(hid_count - 1, -1, -1):
        part = row_piece(hid ^ j, *source, gate_mat, up_mat, piece, bf16 if j else f32)
        source = after(source, part)
        if j:
            received.append(swap(part, "hid", j))
    hidden, d_gate, d_up = after((hidden, d_gate, d_up), part)
    rows_e = whole(own_rows, after(row_parts, part))
    grads_e = whole(own_grads, after(grad_parts, part))
    (grad_gate,) = outer(rows_e, d_gate)
    (grad_down,) = outer(hidden, grads_e)
    if len(received) == 3:
        part = part + received[0].astype(f32)
        received = after(received[1:], part)
    received = after(received, (grad_gate, grad_down))
    block = (capacity, piece + LANES)
    own_sum, *messages = whole_call(
        sum_kernel, "sum_step", [(block, f32)] + [(block, bf16)] * (seq_count - 1), None, part, *received
    )
    (grad_up,) = outer(rows_e, d_up)
    arrived = [swap(message, "seq", k) for k, message in enumerate(messages, 1)]
    for part in after(arrived, grad_up):
        own_sum = own_sum + part.astype(f32)

    half = own_sum.astype(bf16)
    other_half = swap(half, "exp", 1)
    select_other = pick_of((expert_ids == 1 - expert).astype(jnp.int32), capacity).astype(bf16)
    d_tokens, d_gates = whole_call(
        place_kernel,
        "place_step",
        [((tok_rows, piece), f32), ((2, tok_rows), f32)],
        expert,
        expert_ids.T,
        gate_probs.T,
        select_own,
        select_other,
        half,
        other_half,
    )

    return (grad_gate[None], grad_up[None], grad_down[None], d_tokens, d_gates.T)


def solution(mesh):
    return jax.shard_map(
        on_device,
        mesh=mesh,
        in_specs=(
            P("seq", None),
            P("seq", None),
            P("seq", None),
            P("seq", None),
            P("exp", None, ("seq", "hid")),
            P("exp", None, ("seq", "hid")),
            P("exp", ("seq", "hid"), None),
        ),
        out_specs=(
            P("exp", None, ("seq", "hid")),
            P("exp", None, ("seq", "hid")),
            P("exp", ("seq", "hid"), None),
            P("seq", "hid"),
            P("seq", None),
        ),
        check_vma=False,
    )
```
